128 devices in a mesh: tok: 16 (over y, z_hi, core), ch: 8 (over x, z_lo).
Axes of the slice: x: 4, y: 4, z: 4 (z_hi: 2, z_lo: 2; z = z_hi * 2 + z_lo), core: 2. Of those that a mesh axis runs over, the one named last changes fastest.
Arguments:
- inputs: float32 [8192, 2048], P('tok', 'ch'), may hold values from -6 to 6
- cotangent: float32 [8192, 2048], P('tok', 'ch'), may hold values from -6 to 6
- token_in: bfloat16 [2048, 8192], P('tok', 'ch'), may hold values from -0.0625 to 0.0625
- token_out: bfloat16 [8192, 2048], P('tok', 'ch'), may hold values from -0.125 to 0.125
- channel_in: bfloat16 [2048, 6144], P('tok', 'ch'), may hold values from -0.125 to 0.125
- channel_out: bfloat16 [6144, 2048], P('ch', 'tok'), may hold values from -0.078125 to 0.078125
Outputs:
- grad_inputs: float32 [8192, 2048], P('tok', 'ch')
- grad_token_in: float32 [2048, 8192], P('tok', 'ch')
- grad_token_out: float32 [8192, 2048], P('tok', 'ch')
- grad_channel_in: float32 [2048, 6144], P('tok', 'ch')
- grad_channel_out: float32 [6144, 2048], P('ch', 'tok')
The draws below stay inside these ranges and needn't reach their ends.
All inputs are finite; a program needn't handle non-finite values.
Results may differ from the reference program's by a relative error of at most 0.024.
Values may be sent and summed in bfloat16 or wider, within the bound.
No kernel may reach another device: no remote copies, remote signals or barrier semaphores. Data moves between devices by JAX's collectives and lax.ppermute only.
A program may use at most 128 MiB of HBM per device.

```python
import jax
import jax.numpy as jnp
from jax import lax

N = 8192
C = 2048
HT = 2048
HC = 6144
N_TOK = 16
N_CH = 8


def levels(stream_key, extent, pieces, low, top_value):
    loudness = 1.0
    for axis_at, blocks in pieces:
        steps = jax.random.uniform(jax.random.fold_in(jax.random.fold_in(stream_key, 6), axis_at), (blocks,), jnp.float32, low / len(pieces), top_value / len(pieces))
        loudness = loudness * jnp.repeat(jnp.exp(steps), extent[axis_at] // blocks).reshape((-1,) + (1,) * (len(extent) - 1 - axis_at))
    return loudness


def bell_draw(own_key, dims, spread, reach, pieces=(), dtype=jnp.bfloat16):
    loudness = levels(own_key, dims, pieces, -0.22, 0.18) if pieces else 1.0
    entries = jax.random.normal(own_key, dims, jnp.float32) * spread * loudness
    return jnp.minimum(jnp.maximum(entries, -reach), reach).astype(dtype)


def setup_inputs(seed: int = 0) -> dict:
    streams_of = jax.random.split(jax.random.key(seed), 7)
    return {
        "inputs": bell_draw(streams_of[0], (N, C), 1.0, 6.0, ((0, 16), (1, 8)), jnp.float32),
        "cotangent": bell_draw(streams_of[1], (N, C), 1.0, 6.0, ((0, 16), (1, 8)), jnp.float32),
        "token_in": bell_draw(streams_of[2], (HT, N), N ** -0.5, 0.0625, ((0, 16), (1, 8))),
        "token_out": bell_draw(streams_of[3], (N, HT), HT ** -0.5, 0.125, ((0, 16), (1, 8))),
        "channel_in": bell_draw(streams_of[4], (C, HC), C ** -0.5, 0.125, ((0, 16), (1, 8))),
        "channel_out": bell_draw(streams_of[5], (HC, C), HC ** -0.5, 0.078125, ((0, 8), (1, 16))),
    }


GELU_SCALE = 0.7978845608028654
CUBIC = 0.044715
EPSILON = 1e-05

def gelu_forward(value):
    inner = jnp.tanh(GELU_SCALE * (value + CUBIC * value * value * value))
    return 0.5 * value * (1.0 + inner)

def gelu_slope(value):
    inner = jnp.tanh(GELU_SCALE * (value + CUBIC * value * value * value))
    return 0.5 * (1.0 + inner) + 0.5 * value * (1.0 - inner * inner) * GELU_SCALE * (1.0 + 3.0 * CUBIC * value * value)

def norm_rows(values):
    mean = lax.optimization_barrier(jnp.sum(values, axis=1)) / C
    inverse = lax.rsqrt(lax.optimization_barrier(jnp.sum(values * values, axis=1)) / C - mean * mean + EPSILON)
    return ((values - mean[:, None]) * inverse[:, None], inverse)

def norm_adjoint(grad, normed, inverse):
    first = lax.optimization_barrier(jnp.sum(grad, axis=1)) / C
    second = lax.optimization_barrier(jnp.sum(grad * normed, axis=1)) / C
    return inverse[:, None] * (grad - first[:, None] - normed * second[:, None])

def contract(left, right, left_dim, right_dim):
    return lax.dot_general(left, right, (((left_dim,), (right_dim,)), ((), ())), preferred_element_type=jnp.float32)

def blocked(term, count, shape):

    def step(index, total):
        part = term(index).astype(jnp.bfloat16)
        part = lax.optimization_barrier(part)
        return total + part.astype(jnp.float32)
    return lax.fori_loop(0, count, step, jnp.zeros(shape, jnp.float32))

def slice_of(array, index, width, axis):
    start = (index * width).astype(jnp.int32)
    return lax.dynamic_slice_in_dim(array, start, width, axis)

def reference(inputs, cotangent, token_in, token_out, channel_in, channel_out):
    tok_width = N // N_TOK
    ch_width = C // N_CH
    hc_width = HC // N_CH
    first_normed, first_inverse = norm_rows(inputs)
    first_rounded = first_normed.astype(jnp.bfloat16)
    token_pre = jnp.dot(token_in, first_rounded, preferred_element_type=jnp.float32)
    token_act = gelu_forward(token_pre).astype(jnp.bfloat16)
    middle = inputs + jnp.dot(token_out, token_act, preferred_element_type=jnp.float32)
    second_normed, second_inverse = norm_rows(middle)
    second_rounded = second_normed.astype(jnp.bfloat16)
    channel_pre = jnp.dot(second_rounded, channel_in, preferred_element_type=jnp.float32)
    channel_act = gelu_forward(channel_pre).astype(jnp.bfloat16)
    grad_rounded = cotangent.astype(jnp.bfloat16)
    grad_act = contract(grad_rounded, channel_out, 1, 1)
    grad_channel_out = blocked(lambda i: contract(slice_of(channel_act, i, tok_width, 0), slice_of(grad_rounded, i, tok_width, 0), 0, 0), N_TOK, (HC, C))
    grad_pre = (grad_act * gelu_slope(channel_pre)).astype(jnp.bfloat16)
    grad_channel_in = blocked(lambda i: contract(slice_of(second_rounded, i, tok_width, 0), slice_of(grad_pre, i, tok_width, 0), 0, 0), N_TOK, (C, HC))
    grad_second = blocked(lambda i: contract(slice_of(grad_pre, i, hc_width, 1), slice_of(channel_in, i, hc_width, 1), 1, 1), N_CH, (N, C))
    grad_middle = cotangent + norm_adjoint(grad_second, second_normed, second_inverse)
    middle_rounded = grad_middle.astype(jnp.bfloat16)
    grad_token_act = blocked(lambda i: contract(slice_of(token_out, i, tok_width, 0), slice_of(middle_rounded, i, tok_width, 0), 0, 0), N_TOK, (HT, C))
    grad_token_out = blocked(lambda i: contract(slice_of(middle_rounded, i, ch_width, 1), slice_of(token_act, i, ch_width, 1), 1, 1), N_CH, (N, HT))
    token_grad_pre = (grad_token_act * gelu_slope(token_pre)).astype(jnp.bfloat16)
    grad_token_in = blocked(lambda i: contract(slice_of(token_grad_pre, i, ch_width, 1), slice_of(first_rounded, i, ch_width, 1), 1, 1), N_CH, (HT, N))
    grad_first = contract(token_in, token_grad_pre, 0, 0)
    grad_inputs = grad_middle + norm_adjoint(grad_first, first_normed, first_inverse)
    return (grad_inputs, grad_token_in, grad_token_out, grad_channel_in, grad_channel_out)
```

```python
import jax
import jax.numpy as jnp
from jax import lax
from jax.experimental import pallas as pl
from jax.experimental.pallas import tpu as pltpu
from jax.sharding import PartitionSpec as P

C = 2048
GELU_SCALE = 0.7978845608028654
CUBIC = 0.044715
EPSILON = 1e-05
BF = jnp.bfloat16
F32 = jnp.float32


def gelu_forward(value):
    inner = jnp.tanh(GELU_SCALE * (value + CUBIC * value * value * value))
    return 0.5 * value * (1.0 + inner)


def gelu_slope(value):
    inner = jnp.tanh(GELU_SCALE * (value + CUBIC * value * value * value))
    return 0.5 * (1.0 + inner) + 0.5 * value * (1.0 - inner * inner) * GELU_SCALE * (
        1.0 + 3.0 * CUBIC * value * value
    )


def finish_norm(values, total, total_sq):
    mean = total / C
    inverse = lax.rsqrt(total_sq / C - mean * mean + EPSILON)
    return ((values - mean[:, None]) * inverse[:, None], inverse)


def finish_adjoint(grad, normed, inverse, first_sum, second_sum):
    return inverse[:, None] * (grad - (first_sum / C)[:, None] - normed * (second_sum / C)[:, None])


def dot(left, right, left_dim=1, right_dim=0):
    return lax.dot_general(
        left, right, (((left_dim,), (right_dim,)), ((), ())), preferred_element_type=F32
    )


def ch_xor(x, k):
    return lax.ppermute(x, "ch", [(i, i ^ k) for i in range(8)])


def tok_xor(x, k):
    return lax.ppermute(x, "tok", [(i, i ^ k) for i in range(16)])


def gather_ch(x):
    return [x] + [ch_xor(x, k) for k in range(1, 8)]


def gather_tok(x):
    own = [x] + [tok_xor(x, 2 * j) for j in range(1, 8)]
    return own + [tok_xor(block, 1) for block in own]


def scatter_ch(parts):
    total = parts[0].astype(F32)
    for k in range(1, 8):
        total = total + ch_xor(parts[k], k).astype(F32)
    return total


def scatter_tok(keep, send):
    both = (keep.astype(F32) + tok_xor(send, 1).astype(F32)).astype(BF)
    total = both[0].astype(F32)
    for j in range(1, 8):
        total = total + tok_xor(both[j], 2 * j).astype(F32)
    return total


def sum_ch(first, second):
    block = jnp.stack([first, second])
    spread = jnp.broadcast_to(block[None], (8,) + block.shape)
    total = jnp.sum(lax.all_to_all(spread, "ch", 0, 0, tiled=True), axis=0)
    return total[0], total[1]


ANY = pl.BlockSpec(memory_space=pl.ANY)
VM = pl.BlockSpec(memory_space=pltpu.VMEM)


def call(kernel, name, ins, in_specs, outs, scratch, n_copies, flops):
    moved = sum(x.size * x.dtype.itemsize for x in ins) + sum(
        o.size * o.dtype.itemsize for o in outs
    )
    return pl.pallas_call(
        kernel,
        name=name,
        out_shape=outs,
        in_specs=in_specs,
        out_specs=[VM] * len(outs),
        scratch_shapes=list(scratch) + [pltpu.SemaphoreType.DMA((n_copies,))],
        cost_estimate=pl.CostEstimate(flops=flops, bytes_accessed=moved, transcendentals=0),
    )(*ins)


def where_am_i():
    me = lax.axis_index("ch")
    tok = lax.axis_index("tok")
    return me, tok // 2, tok % 2


def fetch(pairs, sems):
    copies = [pltpu.make_async_copy(src, dst, sems.at[n]) for n, (src, dst) in enumerate(pairs)]
    for copy in copies:
        copy.start()
    for copy in copies:
        copy.wait()


def ch_pairs(blocks, scratch, me):
    return [(blocks[k], scratch.at[me ^ k]) for k in range(8)]


def ch_column_pairs(blocks, scratch, me):
    return [
        (blocks[k], scratch.at[:, pl.ds(pl.multiple_of((me ^ k) * 256, 256), 256)])
        for k in range(8)
    ]


def tok_pairs(blocks, scratch, pair, core):
    return [
        (blocks[8 * s + j], scratch.at[(pair ^ j) * 2 + (core ^ s)])
        for s in range(2)
        for j in range(8)
    ]


def token_pre_kernel(*refs):
    rows, normed = refs[:8], refs[8:24]
    pre_ref, act_ref, row_all, normed_all, sems = refs[24:]
    me, pair, core = where_am_i()
    fetch(ch_pairs(rows, row_all, me) + tok_pairs(normed, normed_all, pair, core), sems)
    total = jnp.zeros((128, 256), F32)
    for c in range(8):
        total = total + dot(row_all[c], normed_all[2 * c : 2 * c + 2].reshape(1024, 256))
    pre_ref[...] = total
    act_ref[...] = gelu_forward(total).astype(BF)


def middle_kernel(*refs):
    out_blocks, act_blocks, inputs_ref = refs[:8], refs[8:24], refs[24]
    middle_ref, out_all, act_all, sems = refs[25:]
    me, pair, core = where_am_i()
    fetch(
        ch_column_pairs(out_blocks, out_all, me) + tok_pairs(act_blocks, act_all, pair, core), sems
    )
    middle_ref[...] = inputs_ref[...] + dot(out_all[...], act_all[...].reshape(2048, 256))


def channel_kernel(*refs):
    normed, grads, weights = refs[:8], refs[8:16], refs[16]
    act_ref, pre_ref = refs[17:19]
    parts = refs[19:27]
    normed_all, grad_all, weight_all, sems = refs[27:]
    me, _, _ = where_am_i()
    fetch(
        ch_column_pairs(normed, normed_all, me)
        + ch_column_pairs(grads, grad_all, me)
        + [(weights, weight_all)],
        sems,
    )
    for h in range(3):
        cols = slice(256 * h, 256 * h + 256)
        pre = dot(normed_all[...], weight_all[:, cols])
        grad_act = dot(grad_all[...], weight_all[:, 768 + 256 * h : 1024 + 256 * h])
        act_ref[:, cols] = gelu_forward(pre).astype(BF)
        pre_ref[:, cols] = (grad_act * gelu_slope(pre)).astype(BF)
    for k in range(8):
        rows = pl.ds(pl.multiple_of((me ^ k) * 256, 256), 256)
        parts[k][...] = dot(pre_ref[...], weight_all[rows, :768], 1, 1).astype(BF)


def channel_grad_kernel(*refs):
    normed, grads = refs[:8], refs[8:16]
    act_ref, pre_ref, out_ref, sems = refs[16:]
    me, _, _ = where_am_i()
    for k in range(8):
        rows = pl.ds(pl.multiple_of((me ^ k) * 256, 256), 256)
        out_ref[rows, :768] = dot(normed[k][...], pre_ref[...], 0, 0).astype(BF)
        out_ref[rows, 768:] = dot(grads[k][...], act_ref[...], 0, 0).astype(BF)


def token_act_grad_kernel(*refs):
    out_blocks, middle_ref = refs[:8], refs[8]
    keep_ref, send_ref, sems = refs[9:]
    me, pair, core = where_am_i()
    for k in range(8):
        block = dot(out_blocks[k][...], middle_ref[...], 0, 0).astype(BF)
        low, high = block[:128], block[128:]
        j = me ^ k ^ pair
        first = core == 0
        keep_ref[j] = jnp.where(first, low, high)
        send_ref[j] = jnp.where(first, high, low)


def token_out_kernel(*refs):
    act_blocks, middle_ref = refs[:16], refs[16]
    parts = refs[17:25]
    act_all, sems = refs[25:]
    me, pair, core = where_am_i()
    fetch(tok_pairs(act_blocks, act_all, pair, core), sems)
    for k in range(8):
        block = act_all[pl.ds((me ^ k) * 2, 2)].reshape(256, 256)
        parts[k][...] = dot(middle_ref[...], block, 1, 1).astype(BF)


def token_in_kernel(*refs):
    normed, grad_ref = refs[:16], refs[16]
    parts = refs[17:25]
    normed_all, sems = refs[25:]
    me, pair, core = where_am_i()
    fetch(tok_pairs(normed, normed_all, pair, core), sems)
    for k in range(8):
        block = normed_all[pl.ds((me ^ k) * 2, 2)].reshape(1024, 256)
        parts[k][...] = dot(grad_ref[...], block, 1, 1).astype(BF)


def grad_first_kernel(*refs):
    grads, columns_ref = refs[:16], refs[16]
    out_ref, grad_all, sems = refs[17:]
    me, pair, core = where_am_i()
    fetch(tok_pairs(grads, grad_all, pair, core), sems)
    out_ref[...] = dot(columns_ref[...], grad_all[...].reshape(2048, 256), 0, 0)


def shape(dims, dtype=BF):
    return jax.ShapeDtypeStruct(dims, dtype)


def body(inputs, cotangent, token_in, token_out, channel_in, channel_out):
    weights = lax.all_gather(
        jnp.concatenate([channel_in, channel_out.T], axis=1), "tok", axis=0, tiled=True
    )
    row_total, row_square = sum_ch(jnp.sum(inputs, axis=1), jnp.sum(inputs * inputs, axis=1))
    first_normed, first_inverse = finish_norm(inputs, row_total, row_square)
    first_rounded = first_normed.astype(BF)
    normed_cols = gather_tok(first_rounded)
    in_rows = gather_ch(token_in)
    out_rows = gather_ch(token_out)
    grad_rounded = cotangent.astype(BF)

    core = lax.axis_index("tok") % 2
    halves = token_in[:, :512], token_in[:, 512:]
    mine = jnp.where(core == 0, halves[0], halves[1])
    other = tok_xor(jnp.where(core == 0, halves[1], halves[0]), 1)
    pair_rows = jnp.where(
        core == 0, jnp.concatenate([mine, other]), jnp.concatenate([other, mine])
    )
    flip = []
    for t in range(16):
        for c in range(8):
            flip.append((t * 8 + c, (2 * c + t % 2) * 8 + t // 2))
    own_block = lax.ppermute(pair_rows, ("tok", "ch"), flip)
    own_columns = lax.all_gather(own_block, "ch", axis=0, tiled=True)

    token_pre, token_act = call(
        token_pre_kernel, "token_pre", in_rows + normed_cols, [ANY] * 24,
        [shape((128, 256), F32), shape((128, 256))],
        [pltpu.VMEM((8, 128, 1024), BF), pltpu.VMEM((16, 512, 256), BF)], 24, 2 * 128 * 8192 * 256,
    )
    acts = gather_tok(token_act)
    grad_wide = gather_ch(grad_rounded)
    (middle,) = call(
        middle_kernel, "middle", out_rows + acts + [inputs], [ANY] * 24 + [VM],
        [shape((512, 256), F32)],
        [pltpu.VMEM((512, 2048), BF), pltpu.VMEM((16, 128, 256), BF)], 24, 2 * 512 * 2048 * 256,
    )
    mid_total, mid_square = sum_ch(jnp.sum(middle, axis=1), jnp.sum(middle * middle, axis=1))
    second_normed, second_inverse = finish_norm(middle, mid_total, mid_square)
    normed_wide = gather_ch(second_normed.astype(BF))
    results = call(
        channel_kernel, "channel", normed_wide + grad_wide + [weights], [ANY] * 17,
        [shape((512, 768)), shape((512, 768))] + [shape((512, 256))] * 8,
        [pltpu.VMEM((512, 2048), BF), pltpu.VMEM((512, 2048), BF), pltpu.VMEM((2048, 1536), BF)],
        17, 6 * 512 * 2048 * 768,
    )
    channel_act, grad_pre, parts_second = results[0], results[1], results[2:]
    (part_channel,) = call(
        channel_grad_kernel, "channel_grad",
        normed_wide + grad_wide + [channel_act, grad_pre], [VM] * 18,
        [shape((2048, 1536))], [], 1, 4 * 512 * 2048 * 768,
    )
    grad_channel = lax.psum_scatter(part_channel, "tok", scatter_dimension=0, tiled=True)
    grad_second = scatter_ch(parts_second)
    adj_first, adj_second = sum_ch(
        jnp.sum(grad_second, axis=1), jnp.sum(grad_second * second_normed, axis=1)
    )
    grad_middle = cotangent + finish_adjoint(
        grad_second, second_normed, second_inverse, adj_first, adj_second
    )
    middle_rounded = grad_middle.astype(BF)
    keep, send = call(
        token_act_grad_kernel, "token_act_grad", out_rows + [middle_rounded], [VM] * 9,
        [shape((8, 128, 256))] * 2, [], 1, 2 * 512 * 2048 * 256,
    )
    grad_token_act = scatter_tok(keep, send)
    parts_out = call(
        token_out_kernel, "token_out", acts + [middle_rounded], [ANY] * 16 + [VM],
        [shape((512, 256))] * 8, [pltpu.VMEM((16, 128, 256), BF)], 16, 2 * 512 * 2048 * 256,
    )
    grad_token_out = scatter_ch(parts_out)
    token_grad_pre = (grad_token_act * gelu_slope(token_pre)).astype(BF)
    pre_all = gather_tok(token_grad_pre)
    parts_in = call(
        token_in_kernel, "token_in", normed_cols + [token_grad_pre], [ANY] * 16 + [VM],
        [shape((128, 1024))] * 8, [pltpu.VMEM((16, 512, 256), BF)], 16, 2 * 128 * 8192 * 256,
    )
    grad_token_in = scatter_ch(parts_in)
    (grad_first,) = call(
        grad_first_kernel, "grad_first", pre_all + [own_columns], [ANY] * 16 + [VM],
        [shape((512, 256), F32)], [pltpu.VMEM((16, 128, 256), BF)], 16, 2 * 512 * 2048 * 256,
    )
    last_first, last_second = sum_ch(
        jnp.sum(grad_first, axis=1), jnp.sum(grad_first * first_normed, axis=1)
    )
    grad_inputs = grad_middle + finish_adjoint(
        grad_first, first_normed, first_inverse, last_first, last_second
    )
    grad_channel_in = grad_channel[:, :768].astype(F32)
    grad_channel_out = grad_channel[:, 768:].T.astype(F32)
    return (grad_inputs, grad_token_in, grad_token_out, grad_channel_in, grad_channel_out)


def solution(mesh):
    return jax.shard_map(
        body,
        mesh=mesh,
        in_specs=(
            P("tok", "ch"),
            P("tok", "ch"),
            P("tok", "ch"),
            P("tok", "ch"),
            P("tok", "ch"),
            P("ch", "tok"),
        ),
        out_specs=(P("tok", "ch"), P("tok", "ch"), P("tok", "ch"), P("tok", "ch"), P("ch", "tok")),
        check_vma=False,
    )
```

```python
import jax
import jax.numpy as jnp
from jax import lax
from jax.experimental import pallas as pl
from jax.experimental.pallas import tpu as pltpu
from jax.sharding import PartitionSpec as P

C = 2048
GELU_SCALE = 0.7978845608028654
CUBIC = 0.044715
EPSILON = 1e-05
BF = jnp.bfloat16
F32 = jnp.float32


def gelu_forward(value):
    inner = jnp.tanh(GELU_SCALE * (value + CUBIC * value * value * value))
    return 0.5 * value * (1.0 + inner)


def gelu_slope(value):
    inner = jnp.tanh(GELU_SCALE * (value + CUBIC * value * value * value))
    return 0.5 * (1.0 + inner) + 0.5 * value * (1.0 - inner * inner) * GELU_SCALE * (
        1.0 + 3.0 * CUBIC * value * value
    )


def finish_norm(values, total, total_sq):
    mean = total / C
    inverse = lax.rsqrt(total_sq / C - mean * mean + EPSILON)
    return ((values - mean[:, None]) * inverse[:, None], inverse)


def finish_adjoint(grad, normed, inverse, first_sum, second_sum):
    return inverse[:, None] * (grad - (first_sum / C)[:, None] - normed * (second_sum / C)[:, None])


def dot(left, right, left_dim=1, right_dim=0):
    return lax.dot_general(
        left, right, (((left_dim,), (right_dim,)), ((), ())), preferred_element_type=F32
    )


def ch_xor(x, k):
    return lax.ppermute(x, "ch", [(i, i ^ k) for i in range(8)])


def tok_xor(x, k):
    return lax.ppermute(x, "tok", [(i, i ^ k) for i in range(16)])


def after(x, *others):
    return lax.optimization_barrier((x,) + others)[0]


def gather_ch(x):
    near = ch_xor(x, 1)
    blocks = [x, near] + [None] * 6
    for k in (2, 6, 4):
        blocks[k] = ch_xor(x, k)
    for k in (2, 6, 4):
        blocks[k + 1] = ch_xor(near, k)
    return blocks


def gather_pairs(x):
    near = tok_xor(x, 2)
    blocks = [x, near] + [None] * 6
    for j in (2, 6, 4):
        blocks[j] = tok_xor(x, 2 * j)
    for j in (2, 6, 4):
        blocks[j + 1] = tok_xor(near, 2 * j)
    return blocks


def gather_tok(x):
    own = gather_pairs(x)
    return own + [tok_xor(block, 1) for block in own]


def gather_tok_small(x):
    own = gather_pairs(x)
    stacked = jnp.stack(own)
    return [stacked, tok_xor(stacked, 1)]


def scatter_ch(parts):
    moved = [None] * 8
    for k in (1, 2, 6, 3, 7, 4, 5):
        moved[k] = ch_xor(parts[k], k)
    total = parts[0].astype(F32)
    for k in range(1, 8):
        total = total + moved[k].astype(F32)
    return total


CHIPS = [[2 * j + c for j in range(8)] for c in range(2)]


def scatter_tok(keep, send):
    both = (keep.astype(F32) + tok_xor(send, 1).astype(F32)).astype(BF)
    moved = lax.all_to_all(both, "tok", 0, 0, tiled=True, axis_index_groups=CHIPS)
    return jnp.sum(moved.astype(F32), axis=0)


def sum_ch(stats):
    total = jnp.sum(lax.all_to_all(stats, "ch", 0, 0, tiled=True), axis=0)
    return total[0], total[1]


ANY = pl.BlockSpec(memory_space=pl.ANY)
VM = pl.BlockSpec(memory_space=pltpu.VMEM)


def call(kernel, name, ins, in_specs, outs, out_specs, scratch, n_copies, flops):
    moved = sum(x.size * x.dtype.itemsize for x in ins) + sum(
        o.size * o.dtype.itemsize for o in outs
    )
    return pl.pallas_call(
        kernel,
        name=name,
        out_shape=outs,
        in_specs=in_specs,
        out_specs=out_specs,
        scratch_shapes=list(scratch) + [pltpu.SemaphoreType.DMA((n_copies,))],
        cost_estimate=pl.CostEstimate(flops=flops, bytes_accessed=moved, transcendentals=0),
    )(*ins)


def where_am_i():
    me = lax.axis_index("ch")
    tok = lax.axis_index("tok")
    return me, tok // 2, tok % 2


def start(pairs, sems, first=0):
    copies = [
        pltpu.make_async_copy(src, dst, sems.at[first + n]) for n, (src, dst) in enumerate(pairs)
    ]
    for copy in copies:
        copy.start()
    return copies


def fetch(pairs, sems):
    for copy in start(pairs, sems):
        copy.wait()


def ch_pairs(blocks, scratch, me):
    return [(blocks[k], scratch.at[me ^ k]) for k in range(8)]


def back_pairs(scratch, blocks, me):
    return [(scratch.at[me ^ k], blocks[k]) for k in range(8)]


def ch_column_pairs(blocks, scratch, me):
    return [
        (blocks[k], scratch.at[:, pl.ds(pl.multiple_of((me ^ k) * 256, 256), 256)])
        for k in range(8)
    ]


def tok_pairs(blocks, scratch, pair, core):
    return [
        (blocks[8 * s + j], scratch.at[(pair ^ j) * 2 + (core ^ s)])
        for s in range(2)
        for j in range(8)
    ]


def small_pairs(stacks, scratch, pair, core):
    return [
        (stacks[s].at[j], scratch.at[(pair ^ j) * 2 + (core ^ s)])
        for s in range(2)
        for j in range(8)
    ]


def put_stats(ref, first, second):
    ones = jnp.ones((8, 256), F32)
    sums = [
        lax.dot_general(
            ones, value, (((1,), (1,)), ((), ())),
            precision=lax.Precision.HIGHEST, preferred_element_type=F32,
        )
        for value in (first, second)
    ]
    row = lax.broadcasted_iota(jnp.int32, (8, 512), 0)
    block = jnp.where(row == 0, sums[0], sums[1])
    for c in range(8):
        ref[c] = block


def input_stats_kernel(inputs_ref, stats_ref, sems):
    value = inputs_ref[...]
    put_stats(stats_ref, value, value * value)


def token_pre_kernel(*refs):
    rows, normed = refs[:8], refs[8:24]
    pre_ref, act_ref, row_all, normed_all, sems = refs[24:]
    me, pair, core = where_am_i()
    fetch(ch_pairs(rows, row_all, me) + tok_pairs(normed, normed_all, pair, core), sems)

    def step(c, total):
        return total + dot(row_all[c], normed_all[pl.ds(2 * c, 2)].reshape(1024, 256))

    total = lax.fori_loop(0, 8, step, jnp.zeros((128, 256), F32))
    pre_ref[...] = total
    act_ref[...] = gelu_forward(total).astype(BF)


def middle_kernel(*refs):
    out_blocks, act_blocks, inputs_ref = refs[:8], refs[8:10], refs[10]
    middle_ref, stats_ref, out_all, act_all, sems = refs[11:]
    me, pair, core = where_am_i()
    fetch(
        ch_column_pairs(out_blocks, out_all, me) + small_pairs(act_blocks, act_all, pair, core),
        sems,
    )
    middle = inputs_ref[...] + dot(out_all[...], act_all[...].reshape(2048, 256))
    middle_ref[...] = middle
    put_stats(stats_ref, middle, middle * middle)


def channel_kernel(*refs):
    normed, grads, weights = refs[:8], refs[8:16], refs[16]
    act_ref, pre_ref, stats_ref = refs[17:20]
    parts = refs[20:28]
    normed_all, grad_all, weight_all, part_all, first_sum, second_sum, sems = refs[28:]
    me, _, _ = where_am_i()
    fetch(
        ch_column_pairs(normed, normed_all, me)
        + ch_column_pairs(grads, grad_all, me)
        + [(weights, weight_all)],
        sems,
    )

    def hidden(h, carry):
        cols = pl.ds(pl.multiple_of(256 * h, 256), 256)
        pre = dot(normed_all[...], weight_all[:, cols])
        grad_cols = pl.ds(pl.multiple_of(768 + 256 * h, 256), 256)
        grad_act = dot(grad_all[...], weight_all[:, grad_cols])
        act_ref[:, cols] = gelu_forward(pre).astype(BF)
        pre_ref[:, cols] = (grad_act * gelu_slope(pre)).astype(BF)
        return carry

    lax.fori_loop(0, 3, hidden, 0)
    first_sum[...] = jnp.zeros((512, 256), F32)
    second_sum[...] = jnp.zeros((512, 256), F32)

    def part(c, carry):
        rows = pl.ds(pl.multiple_of(c * 256, 256), 256)
        value = dot(pre_ref[...], weight_all[rows, :768], 1, 1).astype(BF)
        part_all[c] = value
        value = value.astype(F32)
        first_sum[...] += value
        second_sum[...] += value * normed_all[:, rows].astype(F32)
        return carry

    lax.fori_loop(0, 8, part, 0)
    copies = start(back_pairs(part_all, parts, me), sems)
    put_stats(stats_ref, first_sum[...], second_sum[...])
    for copy in copies:
        copy.wait()


def channel_grad_kernel(*refs):
    normed, grads = refs[:8], refs[8:16]
    act_ref, pre_ref, out_ref, normed_all, grad_all, sems = refs[16:]
    me, _, _ = where_am_i()
    fetch(ch_pairs(normed, normed_all, me) + ch_pairs(grads, grad_all, me), sems)

    def step(c, carry):
        rows = pl.ds(pl.multiple_of(c * 256, 256), 256)
        out_ref[rows, :768] = dot(normed_all[c], pre_ref[...], 0, 0).astype(BF)
        out_ref[rows, 768:] = dot(grad_all[c], act_ref[...], 0, 0).astype(BF)
        return carry

    lax.fori_loop(0, 8, step, 0)


def token_act_grad_kernel(*refs):
    out_blocks, middle_ref = refs[:8], refs[8]
    keep_ref, send_ref, out_all, sems = refs[9:]
    me, pair, core = where_am_i()
    fetch(ch_pairs(out_blocks, out_all, me), sems)

    def step(c, carry):
        block = dot(out_all[c], middle_ref[...], 0, 0).astype(BF)
        low, high = block[:128], block[128:]
        first = core == 0
        keep_ref[c] = jnp.where(first, low, high)
        send_ref[c] = jnp.where(first, high, low)
        return carry

    lax.fori_loop(0, 8, step, 0)


def token_out_kernel(*refs):
    act_blocks, middle_ref = refs[:2], refs[2]
    parts = refs[3:11]
    act_all, part_all, sems = refs[11:]
    me, pair, core = where_am_i()
    fetch(small_pairs(act_blocks, act_all, pair, core), sems)

    def step(c, carry):
        block = act_all[pl.ds(2 * c, 2)].reshape(256, 256)
        part_all[c] = dot(middle_ref[...], block, 1, 1).astype(BF)
        return carry

    lax.fori_loop(0, 8, step, 0)
    fetch(back_pairs(part_all, parts, me), sems)


def token_in_kernel(*refs):
    normed, grad_ref = refs[:16], refs[16]
    parts = refs[17:25]
    normed_all, part_all, sems = refs[25:]
    me, pair, core = where_am_i()
    fetch(tok_pairs(normed, normed_all, pair, core), sems)

    def step(c, carry):
        block = normed_all[pl.ds(2 * c, 2)].reshape(1024, 256)
        part_all[c] = dot(grad_ref[...], block, 1, 1).astype(BF)
        return carry

    lax.fori_loop(0, 8, step, 0)
    fetch(back_pairs(part_all, parts, me), sems)


def grad_first_kernel(*refs):
    grads, columns, normed_ref = refs[:2], refs[2:10], refs[10]
    out_ref, stats_ref, grad_all, column_all, sems = refs[11:]
    me, pair, core = where_am_i()
    fetch(ch_pairs(columns, column_all, me) + small_pairs(grads, grad_all, pair, core), sems)
    total = dot(column_all[...].reshape(2048, 512), grad_all[...].reshape(2048, 256), 0, 0)
    out_ref[...] = total
    put_stats(stats_ref, total, total * normed_ref[...])


def shape(dims, dtype=BF):
    return jax.ShapeDtypeStruct(dims, dtype)


STATS = shape((8, 8, 512), F32)
WIDE = pltpu.VMEM((512, 2048), BF)
EIGHT = pltpu.VMEM((8, 512, 256), BF)
HIDDEN = pltpu.VMEM((16, 128, 256), BF)
TOKENS = pltpu.VMEM((16, 512, 256), BF)


def body(inputs, cotangent, token_in, token_out, channel_in, channel_out):
    (stats,) = call(
        input_stats_kernel, "input_stats", [inputs], [VM], [STATS], [VM], [], 1, 2 * 10**6
    )
    row_total, row_square = sum_ch(stats)
    first_normed, first_inverse = finish_norm(inputs, row_total, row_square)
    normed_cols = gather_tok(first_normed.astype(BF))
    in_rows = gather_ch(token_in)
    out_rows = gather_ch(after(token_out, in_rows[3], in_rows[7]))
    grad_wide = gather_ch(after(cotangent.astype(BF), out_rows[3], out_rows[7]))

    own_weights = jnp.concatenate([channel_in, channel_out.T], axis=1)
    weights = lax.all_gather(
        after(own_weights, normed_cols[3], normed_cols[7]), "tok", axis=0, tiled=True
    )

    core = lax.axis_index("tok") % 2
    halves = token_in[:, :512], token_in[:, 512:]
    mine = jnp.where(core == 0, halves[0], halves[1])
    other = tok_xor(jnp.where(core == 0, halves[1], halves[0]), 1)
    pair_rows = jnp.where(
        core == 0, jnp.concatenate([mine, other]), jnp.concatenate([other, mine])
    )
    flip = []
    for t in range(16):
        for c in range(8):
            flip.append((t * 8 + c, (2 * c + t % 2) * 8 + t // 2))
    own_block = lax.ppermute(
        after(pair_rows, normed_cols[3], normed_cols[7]), ("tok", "ch"), flip
    )

    token_pre, token_act = call(
        token_pre_kernel, "token_pre", in_rows + normed_cols, [ANY] * 24,
        [shape((128, 256), F32), shape((128, 256))], [VM] * 2,
        [pltpu.VMEM((8, 128, 1024), BF), TOKENS], 24, 2 * 128 * 8192 * 256,
    )
    acts = gather_tok_small(token_act)
    middle, stats = call(
        middle_kernel, "middle", out_rows + acts + [inputs], [ANY] * 10 + [VM],
        [shape((512, 256), F32), STATS], [VM] * 2, [WIDE, HIDDEN], 24, 2 * 512 * 2048 * 256,
    )
    mid_total, mid_square = sum_ch(stats)
    second_normed, second_inverse = finish_norm(middle, mid_total, mid_square)
    normed_wide = gather_ch(second_normed.astype(BF))
    results = call(
        channel_kernel, "channel", normed_wide + grad_wide + [weights], [ANY] * 17,
        [shape((512, 768)), shape((512, 768)), STATS] + [shape((512, 256))] * 8,
        [VM] * 3 + [ANY] * 8,
        [WIDE, WIDE, pltpu.VMEM((2048, 1536), BF), EIGHT]
        + [pltpu.VMEM((512, 256), F32)] * 2,
        17, 6 * 512 * 2048 * 768,
    )
    channel_act, grad_pre, stats, parts_second = results[0], results[1], results[2], results[3:]
    adj_first, adj_second = sum_ch(stats)
    grad_second = scatter_ch(parts_second)
    (part_channel,) = call(
        channel_grad_kernel, "channel_grad",
        normed_wide + grad_wide + [channel_act, grad_pre], [ANY] * 16 + [VM] * 2,
        [shape((2048, 1536))], [VM], [EIGHT, EIGHT], 16, 4 * 512 * 2048 * 768,
    )
    grad_channel = lax.psum_scatter(part_channel, "tok", scatter_dimension=0, tiled=True)
    grad_middle = cotangent + finish_adjoint(
        grad_second, second_normed, second_inverse, adj_first, adj_second
    )
    middle_rounded = grad_middle.astype(BF)
    own_columns = gather_ch(after(own_block, middle_rounded))
    keep, send = call(
        token_act_grad_kernel, "token_act_grad", out_rows + [middle_rounded], [ANY] * 8 + [VM],
        [shape((8, 128, 256))] * 2, [VM] * 2, [EIGHT], 8, 2 * 512 * 2048 * 256,
    )
    grad_token_act = scatter_tok(keep, send)
    parts_out = call(
        token_out_kernel, "token_out", acts + [middle_rounded], [ANY] * 2 + [VM],
        [shape((512, 256))] * 8, [ANY] * 8, [HIDDEN, EIGHT], 16, 2 * 512 * 2048 * 256,
    )
    grad_token_out = scatter_ch(parts_out)
    token_grad_pre = (grad_token_act * gelu_slope(token_pre)).astype(BF)
    pre_all = gather_tok_small(token_grad_pre)
    parts_in = call(
        token_in_kernel, "token_in", normed_cols + [token_grad_pre], [ANY] * 16 + [VM],
        [shape((128, 1024))] * 8, [ANY] * 8, [TOKENS, pltpu.VMEM((8, 128, 1024), BF)],
        16, 2 * 128 * 8192 * 256,
    )
    grad_token_in = scatter_ch(parts_in)
    grad_first, stats = call(
        grad_first_kernel, "grad_first", pre_all + own_columns + [first_normed],
        [ANY] * 10 + [VM], [shape((512, 256), F32), STATS], [VM] * 2,
        [HIDDEN, pltpu.VMEM((8, 256, 512), BF)], 24, 2 * 512 * 2048 * 256,
    )
    last_first, last_second = sum_ch(stats)
    grad_inputs = grad_middle + finish_adjoint(
        grad_first, first_normed, first_inverse, last_first, last_second
    )
    grad_channel_in = grad_channel[:, :768].astype(F32)
    grad_channel_out = grad_channel[:, 768:].T.astype(F32)
    return (grad_inputs, grad_token_in, grad_token_out, grad_channel_in, grad_channel_out)


def solution(mesh):
    return jax.shard_map(
        body,
        mesh=mesh,
        in_specs=(
            P("tok", "ch"),
            P("tok", "ch"),
            P("tok", "ch"),
            P("tok", "ch"),
            P("tok", "ch"),
            P("ch", "tok"),
        ),
        out_specs=(P("tok", "ch"), P("tok", "ch"), P("tok", "ch"), P("tok", "ch"), P("ch", "tok")),
        check_vma=False,
    )
```

```python
import jax
import jax.numpy as jnp
from jax import lax
from jax.experimental import pallas as pl
from jax.experimental.pallas import tpu as pltpu
from jax.sharding import PartitionSpec as P


C = 2048
GELU_SCALE = 0.7978845608028654
CUBIC = 0.044715
EPSILON = 1e-05
BF = jnp.bfloat16
F32 = jnp.float32


def gelu_forward(value):
    inner = jnp.tanh(GELU_SCALE * (value + CUBIC * value * value * value))
    return 0.5 * value * (1.0 + inner)


def gelu_slope(value):
    inner = jnp.tanh(GELU_SCALE * (value + CUBIC * value * value * value))
    return 0.5 * (1.0 + inner) + 0.5 * value * (1.0 - inner * inner) * GELU_SCALE * (
        1.0 + 3.0 * CUBIC * value * value
    )


def finish_norm(values, total, total_sq):
    mean = total / C
    inverse = lax.rsqrt(total_sq / C - mean * mean + EPSILON)
    return ((values - mean[:, None]) * inverse[:, None], inverse)


def finish_adjoint(grad, normed, inverse, first_sum, second_sum):
    return inverse[:, None] * (grad - (first_sum / C)[:, None] - normed * (second_sum / C)[:, None])


def dot(left, right, left_dim=1, right_dim=0):
    return lax.dot_general(
        left, right, (((left_dim,), (right_dim,)), ((), ())), preferred_element_type=F32
    )


def ch_xor(x, k):
    return lax.ppermute(x, "ch", [(i, i ^ k) for i in range(8)])


def tok_xor(x, k):
    return lax.ppermute(x, "tok", [(i, i ^ k) for i in range(16)])


def after(x, *others):
    return lax.optimization_barrier((x,) + others)[0]


def relay(x, hop):
    near = hop(x, 1)
    blocks = [x, near] + [None] * 6
    for k in (2, 6, 4):
        blocks[k] = hop(x, k)
    for k in (2, 6, 4):
        blocks[k + 1] = hop(near, k)
    return blocks


def gather_ch(x):
    return relay(x, ch_xor)


def gather_tok(x, groups):
    blocks = relay(x, lambda v, j: tok_xor(v, 2 * j))
    stacks = []
    for group in groups:
        stacked = pack([blocks[j] for j in group])
        stacks += [stacked, tok_xor(stacked, 1)]
    return stacks


def scatter_ch(parts):
    moved = [None] * 8
    for k in (1, 2, 6, 3, 7, 4, 5):
        moved[k] = ch_xor(parts[k], k)
    total = parts[0].astype(F32)
    for k in range(1, 8):
        total = total + moved[k].astype(F32)
    return total


def scatter_ch_far_first(parts):
    moved = [None] * 4
    for i in (1, 3, 2):
        moved[i] = ch_xor(parts[i], 2 * i)
    total = parts[0].astype(F32)
    for i in range(1, 4):
        total = total + moved[i].astype(F32)
    got = ch_xor(total[1].astype(BF), 1)
    return total[0] + got.astype(F32)


CHIPS = [[2 * j + c for j in range(8)] for c in range(2)]


def scatter_tok(keep, send):
    got = tok_xor(send, 1)
    both = (keep.astype(F32) + got.astype(F32)).astype(BF)
    moved = lax.all_to_all(both, "tok", 0, 0, tiled=True, axis_index_groups=CHIPS)
    return jnp.sum(moved.astype(F32), axis=0)


def sum_ch(stats):
    moved = lax.all_to_all(stats, "ch", 0, 0, tiled=True)
    total = jnp.sum(moved, axis=0)
    return total[0], total[1]


ANY = pl.BlockSpec(memory_space=pl.ANY)
VM = pl.BlockSpec(memory_space=pltpu.VMEM)


def call(kernel, ins, in_specs, outs, out_specs, scratch, n_copies, flops):
    moved = sum(x.size * x.dtype.itemsize for x in ins) + sum(
        o.size * o.dtype.itemsize for o in outs
    )
    return pl.pallas_call(
        kernel,
        out_shape=outs,
        in_specs=in_specs,
        out_specs=out_specs,
        scratch_shapes=list(scratch) + [pltpu.SemaphoreType.DMA((n_copies,))],
        cost_estimate=pl.CostEstimate(flops=flops, bytes_accessed=moved, transcendentals=0),
    )(*ins)


def where_am_i():
    me = lax.axis_index("ch")
    tok = lax.axis_index("tok")
    return me, tok // 2, tok % 2


def start(pairs, sems, first=0):
    copies = [
        pltpu.make_async_copy(src, dst, sems.at[first + n]) for n, (src, dst) in enumerate(pairs)
    ]
    for copy in copies:
        copy.start()
    return copies


def fetch(pairs, sems):
    for copy in start(pairs, sems):
        copy.wait()


def ch_pairs(blocks, scratch, me):
    return [(blocks[k], scratch.at[me ^ k]) for k in range(8)]


def back_pairs(scratch, blocks, me):
    return [(scratch.at[me ^ k], blocks[k]) for k in range(8)]


def back_twos(scratch, blocks, me):
    return [(scratch.at[me ^ k], blocks[k // 2].at[k % 2]) for k in range(8)]


def pack_kernel(*refs):
    for n, ref in enumerate(refs[:-2]):
        refs[-2][n] = ref[...]


def pack(blocks):
    out = shape((len(blocks),) + blocks[0].shape)
    return call(pack_kernel, blocks, [VM] * len(blocks), [out], [VM], [], 1, 0)[0]


def weights_kernel(in_ref, out_ref, both_ref, sems):
    both_ref[:, :768] = in_ref[...]
    both_ref[:, 768:] = out_ref[...].T


def ch_column_pairs(blocks, scratch, me):
    return [
        (blocks[k], scratch.at[:, pl.ds(pl.multiple_of((me ^ k) * 256, 256), 256)])
        for k in range(8)
    ]


FIRST_GROUPS = ((0, 2, 6, 4), (1, 3, 7, 5))
SMALL_GROUPS = (tuple(range(8)),)


def tok_pairs(stacks, groups, scratch, pair, core):
    return [
        (stacks[2 * n + s].at[i], scratch.at[(pair ^ j) * 2 + (core ^ s)])
        for n, group in enumerate(groups)
        for s in range(2)
        for i, j in enumerate(group)
    ]


def row_sums(value):
    ones = jnp.ones((256, 128), BF)
    total = jnp.zeros((512, 128), F32)
    for _ in range(3):
        part = value.astype(BF)
        value = value - part.astype(F32)
        total = total + dot(part, ones)
    return total


def put_rows(ref, first, second):
    lane = lax.broadcasted_iota(jnp.int32, (512, 128), 1)
    block = jnp.where(lane == 0, first, second).T[:8]
    for c in range(8):
        ref[c] = block


def put_stats(ref, first, second):
    put_rows(ref, row_sums(first), row_sums(second))


def input_stats_kernel(inputs_ref, stats_ref, sems):
    value = inputs_ref[...]
    put_stats(stats_ref, value, value * value)


def token_pre_kernel(*refs):
    rows, normed = refs[:8], refs[8:12]
    pre_ref, act_ref, blocks_ref, row_all, normed_all, sems = refs[12:]
    me, pair, core = where_am_i()
    fetch(
        ch_pairs(rows, row_all, me) + tok_pairs(normed, FIRST_GROUPS, normed_all, pair, core), sems
    )
    copies = start(
        [
            (row_all.at[t // 2, :, pl.ds(t % 2 * 512, 512)], blocks_ref.at[t])
            for t in range(16)
        ],
        sems,
    )
    total = jnp.zeros((128, 256), F32)
    for c in range(8):
        total = total + dot(row_all[c], normed_all[2 * c : 2 * c + 2].reshape(1024, 256))
    pre_ref[...] = total
    act_ref[...] = gelu_forward(total).astype(BF)
    for copy in copies:
        copy.wait()


def middle_kernel(*refs):
    out_blocks, act_blocks, inputs_ref = refs[:8], refs[8:10], refs[10]
    middle_ref, apart_ref, stats_ref, out_all, act_all, sems = refs[11:]
    me, pair, core = where_am_i()
    fetch(
        ch_column_pairs(out_blocks, out_all, me)
        + tok_pairs(act_blocks, SMALL_GROUPS, act_all, pair, core),
        sems,
    )
    middle = inputs_ref[...] + dot(out_all[...], act_all[...].reshape(2048, 256))
    middle_ref[...] = middle
    mean = row_sums(middle) * (1.0 / 256)
    apart = middle - jnp.concatenate([mean, mean], axis=1)
    apart_ref[...] = apart.astype(BF)
    put_rows(stats_ref, mean, row_sums(apart * apart))


def merge_stats(means, squares):
    mean = jnp.sum(means, axis=0, keepdims=True) * (1.0 / 8)
    apart = means - mean
    total = jnp.sum(squares + 256.0 * apart * apart, axis=0, keepdims=True)
    return mean, lax.rsqrt(total / C + EPSILON)


def grad_act_kernel(*refs):
    grads, weights, out_ref, grad_all, weight_all, sems = refs[:8], *refs[8:]
    me, _, _ = where_am_i()
    fetch(
        ch_column_pairs(grads, grad_all, me) + [(weights.at[:, pl.ds(768, 768)], weight_all)],
        sems,
    )
    for h in range(3):
        cols = slice(256 * h, 256 * h + 256)
        out_ref[:, cols] = dot(grad_all[...], weight_all[:, cols])


def channel_kernel(*refs):
    apart, weights, grad_act_ref, moved_ref = refs[:8], refs[8], refs[9], refs[10]
    act_ref, pre_ref, normed_all, stats_ref = refs[11:15]
    parts = refs[15:23]
    weight_all, first_sum, second_sum, part_all, sems = refs[23:]
    me, _, _ = where_am_i()
    copies = start(
        ch_column_pairs(apart, normed_all, me) + [(weights.at[:, pl.ds(0, 768)], weight_all)],
        sems,
    )
    moved = moved_ref[...]
    means, squares = moved[:, 0], moved[:, 1]
    mean, inverse = merge_stats(means, squares)
    rows = jnp.concatenate(
        [means - mean, jnp.broadcast_to(inverse, (8, 512)), jnp.zeros((112, 512), F32)]
    ).T
    inverse = jnp.broadcast_to(rows[:, 8:9], (512, 256))
    for copy in copies:
        copy.wait()
    for c in range(8):
        cols = slice(256 * c, 256 * c + 256)
        value = normed_all[:, cols].astype(F32) + jnp.broadcast_to(rows[:, c : c + 1], (512, 256))
        normed_all[:, cols] = (value * inverse).astype(BF)

    def hidden(h, carry):
        cols = pl.ds(pl.multiple_of(256 * h, 256), 256)
        pre = dot(normed_all[...], weight_all[:, cols])
        act_ref[:, cols] = gelu_forward(pre).astype(BF)
        pre_ref[:, cols] = (grad_act_ref[:, cols] * gelu_slope(pre)).astype(BF)
        return carry

    lax.fori_loop(0, 3, hidden, 0)
    first_sum[...] = jnp.zeros((512, 256), F32)
    second_sum[...] = jnp.zeros((512, 256), F32)

    def part(c, carry):
        rows = pl.ds(pl.multiple_of(c * 256, 256), 256)
        value = dot(pre_ref[...], weight_all[rows, :], 1, 1).astype(BF)
        part_all[c] = value
        value = value.astype(F32)
        first_sum[...] += value
        second_sum[...] += value * normed_all[:, rows].astype(F32)
        return carry

    lax.fori_loop(0, 8, part, 0)
    copies = start(back_pairs(part_all, parts, me), sems)
    put_stats(stats_ref, first_sum[...], second_sum[...])
    for copy in copies:
        copy.wait()


def channel_grad_kernel(*refs):
    grads, normed_ref = refs[:8], refs[8]
    act_ref, pre_ref, out_ref, grad_all, sems = refs[9:]
    me, _, _ = where_am_i()
    fetch(ch_pairs(grads, grad_all, me), sems)

    def step(c, carry):
        rows = pl.ds(pl.multiple_of(c * 256, 256), 256)
        out_ref[rows, :768] = dot(normed_ref[:, rows], pre_ref[...], 0, 0).astype(BF)
        out_ref[rows, 768:] = dot(grad_all[c], act_ref[...], 0, 0).astype(BF)
        return carry

    lax.fori_loop(0, 8, step, 0)


def token_act_grad_kernel(*refs):
    out_blocks, middle_ref = refs[:8], refs[8]
    keep_ref, send_ref, out_all, sems = refs[9:]
    me, _, core = where_am_i()
    fetch(ch_pairs(out_blocks, out_all, me), sems)

    first = core == 0
    for c in range(8):
        block = dot(out_all[c], middle_ref[...], 0, 0).astype(BF)
        low, high = block[:128], block[128:]
        keep_ref[c] = jnp.where(first, low, high)
        send_ref[c] = jnp.where(first, high, low)


def token_out_kernel(*refs):
    act_blocks, middle_ref = refs[:2], refs[2]
    parts = refs[3:7]
    act_all, part_all, sems = refs[7:]
    me, pair, core = where_am_i()
    fetch(tok_pairs(act_blocks, SMALL_GROUPS, act_all, pair, core), sems)

    for c in range(8):
        block = act_all[2 * c : 2 * c + 2].reshape(256, 256)
        part_all[c] = dot(middle_ref[...], block, 1, 1).astype(BF)
    fetch(back_twos(part_all, parts, me), sems)


def token_in_kernel(*refs):
    normed, grad_ref = refs[:4], refs[4]
    parts = refs[5:9]
    normed_all, part_all, sems = refs[9:]
    me, pair, core = where_am_i()
    fetch(tok_pairs(normed, FIRST_GROUPS, normed_all, pair, core), sems)

    for c in range(8):
        block = normed_all[2 * c : 2 * c + 2].reshape(1024, 256)
        part_all[c] = dot(grad_ref[...], block, 1, 1).astype(BF)
    fetch(back_twos(part_all, parts, me), sems)


def grad_first_kernel(*refs):
    grads, column_ref, normed_ref = refs[:2], refs[2], refs[3]
    out_ref, stats_ref, grad_all, sems = refs[4:]
    _, pair, core = where_am_i()
    fetch(tok_pairs(grads, SMALL_GROUPS, grad_all, pair, core), sems)
    total = dot(column_ref[...], grad_all[...].reshape(2048, 256), 0, 0)
    out_ref[...] = total
    put_stats(stats_ref, total, total * normed_ref[...])


def shape(dims, dtype=BF):
    return jax.ShapeDtypeStruct(dims, dtype)


STATS = shape((8, 8, 512), F32)
WIDE = pltpu.VMEM((512, 2048), BF)
EIGHT = pltpu.VMEM((8, 512, 256), BF)
HIDDEN = pltpu.VMEM((16, 128, 256), BF)
TOKENS = pltpu.VMEM((16, 512, 256), BF)


def body(inputs, cotangent, token_in, token_out, channel_in, channel_out):
    (stats,) = call(input_stats_kernel, [inputs], [VM], [STATS], [VM], [], 1, 2 * 10**6)
    row_total, row_square = sum_ch(stats)
    first_normed, first_inverse = finish_norm(inputs, row_total, row_square)
    normed_cols = gather_tok(first_normed.astype(BF), FIRST_GROUPS)
    in_rows = gather_ch(token_in)
    out_rows = gather_ch(token_out)
    grad_wide = gather_ch(cotangent.astype(BF))

    (own_weights,) = call(
        weights_kernel, [channel_in, channel_out], [VM] * 2,
        [shape((128, 1536))], [VM], [], 1, 0,
    )
    weights = lax.all_gather(after(own_weights, normed_cols[2]), "tok", axis=0, tiled=True)

    token_pre, token_act, row_blocks = call(
        token_pre_kernel, in_rows + normed_cols, [ANY] * 12,
        [shape((128, 256), F32), shape((128, 256)), shape((16, 128, 512))], [VM] * 2 + [ANY],
        [pltpu.VMEM((8, 128, 1024), BF), TOKENS], 24, 2 * 128 * 8192 * 256,
    )
    acts = gather_tok(token_act, SMALL_GROUPS)
    middle, apart, stats = call(
        middle_kernel, out_rows + acts + [inputs], [ANY] * 10 + [VM],
        [shape((512, 256), F32), shape((512, 256)), STATS], [VM] * 3, [WIDE, HIDDEN],
        24, 2 * 512 * 2048 * 256,
    )
    moved = lax.all_to_all(stats, "ch", 0, 0, tiled=True)
    own_columns = lax.all_to_all(row_blocks, "tok", 0, 0, tiled=True).reshape(2048, 512)
    apart_wide = gather_ch(apart)
    (grad_act,) = call(
        grad_act_kernel, grad_wide + [weights], [ANY] * 9,
        [shape((512, 768), F32)], [VM], [WIDE, pltpu.VMEM((2048, 768), BF)],
        9, 2 * 512 * 2048 * 768,
    )
    results = call(
        channel_kernel, apart_wide + [weights, grad_act, moved], [ANY] * 9 + [VM] * 2,
        [shape((512, 768)), shape((512, 768)), shape((512, 2048)), STATS]
        + [shape((512, 256))] * 8,
        [VM] * 4 + [ANY] * 8,
        [pltpu.VMEM((2048, 768), BF)] + [pltpu.VMEM((512, 256), F32)] * 2 + [EIGHT],
        9, 4 * 512 * 2048 * 768,
    )
    channel_act, grad_pre, normed_wide, stats = results[:4]
    parts_second = results[4:]
    adj_first, adj_second = sum_ch(stats)
    grad_second = scatter_ch(parts_second)
    (part_channel,) = call(
        channel_grad_kernel,
        grad_wide + [normed_wide, channel_act, grad_pre], [ANY] * 8 + [VM] * 3,
        [shape((2048, 1536))], [VM], [EIGHT], 8, 4 * 512 * 2048 * 768,
    )
    grad_channel = lax.psum_scatter(part_channel, "tok", scatter_dimension=0, tiled=True)
    mid_mean, mid_inverse = merge_stats(moved[:, 0], moved[:, 1])
    second_inverse = mid_inverse[0]
    second_normed = (middle - mid_mean[0][:, None]) * second_inverse[:, None]
    grad_middle = cotangent + finish_adjoint(
        grad_second, second_normed, second_inverse, adj_first, adj_second
    )
    middle_rounded = grad_middle.astype(BF)
    keep, send = call(
        token_act_grad_kernel, out_rows + [middle_rounded], [ANY] * 8 + [VM],
        [shape((8, 128, 256))] * 2, [VM] * 2, [EIGHT], 8, 2 * 512 * 2048 * 256,
    )
    grad_token_act = scatter_tok(keep, send)
    parts_out = call(
        token_out_kernel, acts + [middle_rounded], [ANY] * 2 + [VM],
        [shape((2, 512, 256))] * 4, [ANY] * 4, [HIDDEN, EIGHT], 16, 2 * 512 * 2048 * 256,
    )
    grad_token_out = scatter_ch_far_first(parts_out)
    token_grad_pre = (grad_token_act * gelu_slope(token_pre)).astype(BF)
    pre_all = gather_tok(token_grad_pre, SMALL_GROUPS)
    parts_in = call(
        token_in_kernel, normed_cols + [token_grad_pre], [ANY] * 4 + [VM],
        [shape((2, 128, 1024))] * 4, [ANY] * 4, [TOKENS, pltpu.VMEM((8, 128, 1024), BF)],
        16, 2 * 128 * 8192 * 256,
    )
    grad_token_in = scatter_ch_far_first(parts_in)
    grad_first, stats = call(
        grad_first_kernel, pre_all + [own_columns, first_normed],
        [ANY] * 2 + [VM] * 2, [shape((512, 256), F32), STATS], [VM] * 2,
        [HIDDEN], 16, 2 * 512 * 2048 * 256,
    )
    last_first, last_second = sum_ch(stats)
    grad_inputs = grad_middle + finish_adjoint(
        grad_first, first_normed, first_inverse, last_first, last_second
    )
    grad_channel_in = grad_channel[:, :768].astype(F32)
    grad_channel_out = grad_channel[:, 768:].T.astype(F32)
    return (grad_inputs, grad_token_in, grad_token_out, grad_channel_in, grad_channel_out)


def solution(mesh):
    return jax.shard_map(
        body,
        mesh=mesh,
        in_specs=(
            P("tok", "ch"),
            P("tok", "ch"),
            P("tok", "ch"),
            P("tok", "ch"),
            P("tok", "ch"),
            P("ch", "tok"),
        ),
        out_specs=(P("tok", "ch"), P("tok", "ch"), P("tok", "ch"), P("tok", "ch"), P("ch", "tok")),
        check_vma=False,
    )
```

```python
import jax
import jax.numpy as jnp
from jax import lax
from jax.experimental import pallas as pl
from jax.experimental.pallas import tpu as pltpu
from jax.sharding import PartitionSpec as P


C = 2048
GELU_SCALE = 0.7978845608028654
CUBIC = 0.044715
EPSILON = 1e-05
BF = jnp.bfloat16
F32 = jnp.float32


def gelu_forward(value):
    inner = jnp.tanh(GELU_SCALE * (value + CUBIC * value * value * value))
    return 0.5 * value * (1.0 + inner)


def gelu_slope(value):
    inner = jnp.tanh(GELU_SCALE * (value + CUBIC * value * value * value))
    return 0.5 * (1.0 + inner) + 0.5 * value * (1.0 - inner * inner) * GELU_SCALE * (
        1.0 + 3.0 * CUBIC * value * value
    )


def finish_norm(values, total, total_sq):
    mean = total / C
    inverse = lax.rsqrt(total_sq / C - mean * mean + EPSILON)
    return ((values - mean[:, None]) * inverse[:, None], inverse)


def finish_adjoint(grad, normed, inverse, first_sum, second_sum):
    return inverse[:, None] * (grad - (first_sum / C)[:, None] - normed * (second_sum / C)[:, None])


def dot(left, right, left_dim=1, right_dim=0):
    return lax.dot_general(
        left, right, (((left_dim,), (right_dim,)), ((), ())), preferred_element_type=F32
    )


def ch_xor(x, k):
    return lax.ppermute(x, "ch", [(i, i ^ k) for i in range(8)])


def tok_xor(x, k):
    return lax.ppermute(x, "tok", [(i, i ^ k) for i in range(16)])


def relay(x, hop):
    near = hop(x, 1)
    blocks = [x, near] + [None] * 6
    for k in (2, 6, 4):
        blocks[k] = hop(x, k)
    for k in (2, 6, 4):
        blocks[k + 1] = hop(near, k)
    return blocks


def gather_ch(x):
    return relay(x, ch_xor)


def gather_tok(x, groups):
    blocks = relay(x, lambda v, j: tok_xor(v, 2 * j))
    stacks = []
    for group in groups:
        stacked = pack([blocks[j] for j in group])
        stacks += [stacked, tok_xor(stacked, 1)]
    return stacks


def scatter_ch(parts):
    moved = [None] * 8
    for k in (1, 2, 6, 3, 7, 4, 5):
        moved[k] = ch_xor(parts[k], k)
    total = parts[0].astype(F32)
    for k in range(1, 8):
        total = total + moved[k].astype(F32)
    return total


def scatter_ch_far_first(parts):
    moved = [None] * 4
    for i in (1, 3, 2):
        moved[i] = ch_xor(parts[i], 2 * i)
    total = parts[0].astype(F32)
    for i in range(1, 4):
        total = total + moved[i].astype(F32)
    got = ch_xor(total[1].astype(BF), 1)
    return total[0] + got.astype(F32)


def gather_small(copies):
    own = lax.all_to_all(copies, "tok", 0, 0, tiled=True, axis_index_groups=CHIPS)
    return [own, tok_xor(own, 1)]


CHIPS = [[2 * j + c for j in range(8)] for c in range(2)]


def reduce_tok(keep, send):
    got = tok_xor(send, 1)
    both = (keep.astype(F32) + got.astype(F32)).astype(BF)
    return lax.all_to_all(both, "tok", 0, 0, tiled=True, axis_index_groups=CHIPS)


def reduce_tok_far_first(keep, send):
    got = tok_xor(send, 1)
    both = [
        (keep[2 * i : 2 * i + 2].astype(F32) + got[2 * i : 2 * i + 2].astype(F32)).astype(BF)
        for i in range(4)
    ]
    moved = [None] * 4
    for i in (1, 3, 2):
        moved[i] = tok_xor(both[i], 4 * i)
    total = both[0].astype(F32)
    for i in range(1, 4):
        total = total + moved[i].astype(F32)
    other = tok_xor(total[1].astype(BF), 2)
    return total[0] + other.astype(F32)


def sum_ch(stats):
    moved = lax.all_to_all(stats, "ch", 0, 0, tiled=True)
    total = jnp.sum(moved, axis=0)
    return total[0], total[1]


ANY = pl.BlockSpec(memory_space=pl.ANY)
VM = pl.BlockSpec(memory_space=pltpu.VMEM)


def call(kernel, ins, in_specs, outs, out_specs, scratch, n_copies, flops):
    moved = sum(x.size * x.dtype.itemsize for x in ins) + sum(
        o.size * o.dtype.itemsize for o in outs
    )
    return pl.pallas_call(
        kernel,
        out_shape=outs,
        in_specs=in_specs,
        out_specs=out_specs,
        scratch_shapes=list(scratch) + [pltpu.SemaphoreType.DMA((n_copies,))],
        cost_estimate=pl.CostEstimate(flops=flops, bytes_accessed=moved, transcendentals=0),
    )(*ins)


def where_am_i():
    me = lax.axis_index("ch")
    tok = lax.axis_index("tok")
    return me, tok // 2, tok % 2


def start(pairs, sems, first=0):
    copies = [
        pltpu.make_async_copy(src, dst, sems.at[first + n]) for n, (src, dst) in enumerate(pairs)
    ]
    for copy in copies:
        copy.start()
    return copies


def fetch(pairs, sems):
    for copy in start(pairs, sems):
        copy.wait()


def ch_pairs(blocks, scratch, me):
    return [(blocks[k], scratch.at[me ^ k]) for k in range(8)]


def back_pairs(scratch, blocks, me):
    return [(scratch.at[me ^ k], blocks[k]) for k in range(8)]


def back_twos(scratch, blocks, me):
    return [(scratch.at[me ^ k], blocks[k // 2].at[k % 2]) for k in range(8)]


def pack_kernel(*refs):
    for n, ref in enumerate(refs[:-2]):
        refs[-2][n] = ref[...]


def pack(blocks):
    out = shape((len(blocks),) + blocks[0].shape)
    return call(pack_kernel, blocks, [VM] * len(blocks), [out], [VM], [], 1, 0)[0]


def weights_kernel(in_ref, out_ref, both_ref, sems):
    both_ref[:, :768] = in_ref[...]
    both_ref[:, 768:] = out_ref[...].T


def ch_column_pairs(blocks, scratch, me):
    return [
        (blocks[k].at[pl.ds(0, 512)], scratch.at[:, pl.ds(pl.multiple_of((me ^ k) * 256, 256), 256)])
        for k in range(8)
    ]


FIRST_GROUPS = ((0, 2, 6, 4), (1, 3, 7, 5))


def small_pairs(stacks, scratch, core):
    return [
        (stacks[s].at[j], scratch.at[2 * j + (core ^ s)]) for s in range(2) for j in range(8)
    ]


def tok_pairs(stacks, groups, scratch, pair, core):
    return [
        (stacks[2 * n + s].at[i], scratch.at[(pair ^ j) * 2 + (core ^ s)])
        for n, group in enumerate(groups)
        for s in range(2)
        for i, j in enumerate(group)
    ]


def row_sums(value):
    ones = jnp.ones((256, 128), BF)
    total = jnp.zeros((512, 128), F32)
    for _ in range(3):
        part = value.astype(BF)
        value = value - part.astype(F32)
        total = total + dot(part, ones)
    return total


def put_rows(ref, first, second):
    lane = lax.broadcasted_iota(jnp.int32, (512, 128), 1)
    block = jnp.where(lane == 0, first, second).T[:8]
    for c in range(8):
        ref[c] = block


def as_tail(first, second):
    lane = lax.broadcasted_iota(jnp.int32, (512, 128), 1)
    value = jnp.where(lane % 2 == 0, first, second).T[:8]
    high = value.astype(BF).astype(F32)
    mid = (value - high).astype(BF).astype(F32)
    row = lax.broadcasted_iota(jnp.int32, (8, 512), 0)
    terms = jnp.where(row < 2, high, jnp.where(row < 4, mid, value - high - mid))
    return jnp.concatenate([terms[:, :256], terms[:, 256:]]).astype(BF)


def from_tail(tail):
    tail = tail.astype(F32)

    def row(n):
        halves = [
            tail[..., at, :] + tail[..., at + 2, :] + tail[..., at + 4, :] for at in (n, n + 8)
        ]
        return jnp.concatenate(halves, axis=-1)

    return row(0), row(1)


def put_stats(ref, first, second):
    put_rows(ref, row_sums(first), row_sums(second))


def input_stats_kernel(inputs_ref, stats_ref, sems):
    value = inputs_ref[...]
    put_stats(stats_ref, value, value * value)


def token_pre_kernel(*refs):
    rows, normed = refs[:8], refs[8:12]
    pre_ref, act_ref, blocks_ref, row_all, normed_all, sems = refs[12:]
    me, pair, core = where_am_i()
    fetch(
        ch_pairs(rows, row_all, me) + tok_pairs(normed, FIRST_GROUPS, normed_all, pair, core), sems
    )
    copies = start(
        [
            (row_all.at[t // 2, :, pl.ds(t % 2 * 512, 512)], blocks_ref.at[t])
            for t in range(16)
        ],
        sems,
    )
    total = jnp.zeros((128, 256), F32)
    for c in range(8):
        total = total + dot(row_all[c], normed_all[2 * c : 2 * c + 2].reshape(1024, 256))
    pre_ref[...] = total
    act = gelu_forward(total).astype(BF)
    for j in range(8):
        act_ref[j] = act
    for copy in copies:
        copy.wait()


def middle_kernel(*refs):
    out_blocks, act_blocks, inputs_ref = refs[:8], refs[8:10], refs[10]
    middle_ref, apart_ref, out_all, act_all, sems = refs[11:]
    me, _, core = where_am_i()
    fetch(
        ch_column_pairs(out_blocks, out_all, me)
        + small_pairs(act_blocks, act_all, core),
        sems,
    )
    middle = inputs_ref[...] + dot(out_all[...], act_all[...].reshape(2048, 256))
    middle_ref[...] = middle
    mean = row_sums(middle) * (1.0 / 256)
    apart = middle - jnp.concatenate([mean, mean], axis=1)
    apart_ref[:512] = apart.astype(BF)
    apart_ref[512:] = as_tail(mean, row_sums(apart * apart))


def merge_stats(means, squares):
    mean = jnp.sum(means, axis=0, keepdims=True) * (1.0 / 8)
    apart = means - mean
    total = jnp.sum(squares + 256.0 * apart * apart, axis=0, keepdims=True)
    return mean, lax.rsqrt(total / C + EPSILON)


def grad_act_kernel(*refs):
    grads, weights, out_ref, grad_all, weight_all, sems = refs[:8], *refs[8:]
    me, _, _ = where_am_i()
    fetch(
        ch_column_pairs(grads, grad_all, me) + [(weights.at[:, pl.ds(768, 768)], weight_all)],
        sems,
    )
    for h in range(3):
        cols = slice(256 * h, 256 * h + 256)
        out_ref[:, cols] = dot(grad_all[...], weight_all[:, cols])


def channel_kernel(*refs):
    apart, weights, grad_act = refs[:8], refs[8], refs[9]
    act_out, pre_out, normed_out, merged_ref = refs[10:14]
    parts = refs[14:22]
    weight_all, first_sum, second_sum, part_all = refs[22:26]
    normed_all, grad_act_ref, act_ref, pre_ref, tails, tail_out, sems = refs[26:]
    me, _, _ = where_am_i()
    first_copies = start(
        [(apart[k].at[pl.ds(512, 16)], tails.at[me ^ k]) for k in range(8)], sems, 13
    )
    copies = start(ch_column_pairs(apart, normed_all, me), sems)
    later = start(
        [(weights.at[:, pl.ds(0, 768)], weight_all), (grad_act, grad_act_ref)], sems, 8
    )
    for copy in first_copies:
        copy.wait()
    means, squares = from_tail(tails[...])
    mean, inverse = merge_stats(means, squares)
    merged_ref[...] = jnp.concatenate([mean, inverse, jnp.zeros((6, 512), F32)])
    rows = jnp.concatenate(
        [means - mean, jnp.broadcast_to(inverse, (8, 512)), jnp.zeros((112, 512), F32)]
    ).T
    inverse = jnp.broadcast_to(rows[:, 8:9], (512, 256))
    for copy in copies:
        copy.wait()
    for c in range(8):
        cols = slice(256 * c, 256 * c + 256)
        value = normed_all[:, cols].astype(F32) + jnp.broadcast_to(rows[:, c : c + 1], (512, 256))
        normed_all[:, cols] = (value * inverse).astype(BF)
    out_copies = start([(normed_all, normed_out)], sems, 10)
    for copy in later:
        copy.wait()

    def hidden(h, carry):
        cols = pl.ds(pl.multiple_of(256 * h, 256), 256)
        pre = dot(normed_all[...], weight_all[:, cols])
        act_ref[:, cols] = gelu_forward(pre).astype(BF)
        pre_ref[:, cols] = (grad_act_ref[:, cols] * gelu_slope(pre)).astype(BF)
        return carry

    lax.fori_loop(0, 3, hidden, 0)
    out_copies += start([(act_ref, act_out), (pre_ref, pre_out)], sems, 11)
    first_sum[...] = jnp.zeros((512, 256), F32)
    second_sum[...] = jnp.zeros((512, 256), F32)

    def part(c, carry):
        rows = pl.ds(pl.multiple_of(c * 256, 256), 256)
        value = dot(pre_ref[...], weight_all[rows, :], 1, 1).astype(BF)
        part_all[c] = value
        value = value.astype(F32)
        first_sum[...] += value
        second_sum[...] += value * normed_all[:, rows].astype(F32)
        return carry

    lax.fori_loop(0, 8, part, 0)
    copies = start(
        [(part_all.at[me ^ k], parts[k].at[pl.ds(0, 512)]) for k in range(8)], sems
    )
    tail_out[...] = as_tail(row_sums(first_sum[...]), row_sums(second_sum[...]))
    copies += start([(tail_out, parts[k].at[pl.ds(512, 16)]) for k in range(8)], sems, 13)
    for copy in copies + out_copies:
        copy.wait()


def channel_grad_kernel(*refs):
    grads, normed_ref = refs[:8], refs[8]
    act_ref, pre_ref, in_ref, keep_ref, send_ref, grad_all, sems = refs[9:]
    me, pair, core = where_am_i()
    fetch(ch_pairs(grads, grad_all, me), sems)
    first = core == 0

    def step(c, carry):
        rows = pl.ds(pl.multiple_of(c * 256, 256), 256)
        in_ref[rows, :] = dot(normed_ref[:, rows], pre_ref[...], 0, 0).astype(BF)
        block = dot(grad_all[c], act_ref[...], 0, 0)
        low, high = block[:128], block[128:]
        keep_ref[c ^ pair] = jnp.where(first, low, high).astype(BF)
        send_ref[c ^ pair] = jnp.where(first, high, low).astype(BF)
        return carry

    lax.fori_loop(0, 8, step, 0)


def widen_kernel(in_ref, out_ref, sems):
    out_ref[...] = in_ref[...].astype(F32)


def keep_kernel(in_ref, out_ref, sems):
    out_ref[...] = in_ref[...]


def token_act_grad_kernel(*refs):
    out_blocks, middle_ref = refs[:8], refs[8]
    keep_ref, send_ref, out_all, sems = refs[9:]
    me, _, core = where_am_i()
    fetch(ch_pairs(out_blocks, out_all, me), sems)

    first = core == 0
    for c in range(8):
        block = dot(out_all[c], middle_ref[...], 0, 0).astype(BF)
        low, high = block[:128], block[128:]
        keep_ref[c] = jnp.where(first, low, high)
        send_ref[c] = jnp.where(first, high, low)


def token_grad_kernel(moved_ref, pre_ref, out_ref, sems):
    total = moved_ref[0].astype(F32)
    for j in range(1, 8):
        total = total + moved_ref[j].astype(F32)
    value = (total * gelu_slope(pre_ref[...])).astype(BF)
    for j in range(8):
        out_ref[j] = value


def token_out_kernel(*refs):
    act_blocks, middle_ref = refs[:2], refs[2]
    parts = refs[3:7]
    act_all, part_all, sems = refs[7:]
    me, _, core = where_am_i()
    fetch(small_pairs(act_blocks, act_all, core), sems)

    for c in range(8):
        block = act_all[2 * c : 2 * c + 2].reshape(256, 256)
        part_all[c] = dot(middle_ref[...], block, 1, 1).astype(BF)
    fetch(back_twos(part_all, parts, me), sems)


def token_in_kernel(*refs):
    normed, grad_ref = refs[:4], refs[4]
    parts = refs[5:13]
    normed_all, part_all, sems = refs[13:]
    me, pair, core = where_am_i()
    fetch(tok_pairs(normed, FIRST_GROUPS, normed_all, pair, core), sems)

    for c in range(8):
        block = normed_all[2 * c : 2 * c + 2].reshape(1024, 256)
        part_all[c] = dot(grad_ref[0], block, 1, 1).astype(BF)
    fetch(back_pairs(part_all, parts, me), sems)


def grad_first_kernel(*refs):
    grads, column_ref, normed_ref = refs[:2], refs[2], refs[3]
    out_ref, stats_ref, grad_all, sems = refs[4:]
    _, _, core = where_am_i()
    fetch(small_pairs(grads, grad_all, core), sems)
    total = dot(column_ref[...], grad_all[...].reshape(2048, 256), 0, 0)
    out_ref[...] = total
    put_stats(stats_ref, total, total * normed_ref[...])


def shape(dims, dtype=BF):
    return jax.ShapeDtypeStruct(dims, dtype)


STATS = shape((8, 8, 512), F32)
WIDE = pltpu.VMEM((512, 2048), BF)
EIGHT = pltpu.VMEM((8, 512, 256), BF)
HIDDEN = pltpu.VMEM((16, 128, 256), BF)
TOKENS = pltpu.VMEM((16, 512, 256), BF)


def body(inputs, cotangent, token_in, token_out, channel_in, channel_out):
    (stats,) = call(input_stats_kernel, [inputs], [VM], [STATS], [VM], [], 1, 2 * 10**6)
    row_total, row_square = sum_ch(stats)
    first_normed, first_inverse = finish_norm(inputs, row_total, row_square)
    normed_cols = gather_tok(first_normed.astype(BF), FIRST_GROUPS)
    in_rows = gather_ch(token_in)
    out_rows = gather_ch(token_out)
    grad_wide = gather_ch(cotangent.astype(BF))

    (own_weights,) = call(
        weights_kernel, [channel_in, channel_out], [VM] * 2,
        [shape((128, 1536))], [VM], [], 1, 0,
    )
    weights = lax.all_gather(own_weights, "tok", axis=0, tiled=True)

    token_pre, token_act, row_blocks = call(
        token_pre_kernel, in_rows + normed_cols, [ANY] * 12,
        [shape((128, 256), F32), shape((8, 128, 256)), shape((16, 128, 512))], [VM] * 2 + [ANY],
        [pltpu.VMEM((8, 128, 1024), BF), TOKENS], 24, 2 * 128 * 8192 * 256,
    )
    acts = gather_small(token_act)
    middle, apart = call(
        middle_kernel, out_rows + acts + [inputs], [ANY] * 10 + [VM],
        [shape((512, 256), F32), shape((528, 256))], [VM] * 2, [WIDE, HIDDEN],
        24, 2 * 512 * 2048 * 256,
    )
    own_columns = lax.all_to_all(row_blocks, "tok", 0, 0, tiled=True).reshape(2048, 512)
    apart_wide = gather_ch(apart)
    (grad_act,) = call(
        grad_act_kernel, grad_wide + [weights], [ANY] * 9,
        [shape((512, 768), F32)], [VM], [WIDE, pltpu.VMEM((2048, 768), BF)],
        9, 2 * 512 * 2048 * 768,
    )
    results = call(
        channel_kernel, apart_wide + [weights, grad_act], [ANY] * 10,
        [shape((512, 768)), shape((512, 768)), shape((512, 2048)), shape((8, 512), F32)]
        + [shape((528, 256))] * 8,
        [ANY] * 3 + [VM] + [ANY] * 8,
        [pltpu.VMEM((2048, 768), BF)] + [pltpu.VMEM((512, 256), F32)] * 2
        + [EIGHT, WIDE, pltpu.VMEM((512, 768), F32)] + [pltpu.VMEM((512, 768), BF)] * 2
        + [pltpu.VMEM((8, 16, 256), BF), pltpu.VMEM((16, 256), BF)],
        21, 4 * 512 * 2048 * 768,
    )
    channel_act, grad_pre, normed_wide, merged = results[:4]
    total_second = scatter_ch(results[4:])
    grad_second = total_second[:512]
    adj_first, adj_second = from_tail(total_second[512:])
    part_in_all, keep_channel, send_channel = call(
        channel_grad_kernel,
        grad_wide + [normed_wide, channel_act, grad_pre], [ANY] * 8 + [VM] * 3,
        [shape((2048, 768))] + [shape((8, 128, 768))] * 2, [VM] * 3, [EIGHT],
        8, 4 * 512 * 2048 * 768,
    )
    grad_channel = lax.psum_scatter(part_in_all, "tok", scatter_dimension=0, tiled=True)
    grad_channel_out = reduce_tok_far_first(keep_channel, send_channel).T
    (merged,) = call(keep_kernel, [merged], [VM], [shape((8, 512), F32)], [VM], [], 1, 0)
    second_inverse = merged[1]
    second_normed = (middle - merged[0][:, None]) * second_inverse[:, None]
    grad_middle = cotangent + finish_adjoint(
        grad_second, second_normed, second_inverse, adj_first, adj_second
    )
    middle_rounded = grad_middle.astype(BF)
    keep, send = call(
        token_act_grad_kernel, out_rows + [middle_rounded], [ANY] * 8 + [VM],
        [shape((8, 128, 256))] * 2, [VM] * 2, [EIGHT], 8, 2 * 512 * 2048 * 256,
    )
    grad_token_act = reduce_tok(keep, send)
    parts_out = call(
        token_out_kernel, acts + [middle_rounded], [ANY] * 2 + [VM],
        [shape((2, 512, 256))] * 4, [ANY] * 4, [HIDDEN, EIGHT], 16, 2 * 512 * 2048 * 256,
    )
    grad_token_out = scatter_ch_far_first(parts_out)
    (token_grad_pre,) = call(
        token_grad_kernel, [grad_token_act, token_pre], [VM] * 2,
        [shape((8, 128, 256))], [VM], [], 1, 0,
    )
    pre_all = gather_small(token_grad_pre)
    parts_in = call(
        token_in_kernel, normed_cols + [token_grad_pre], [ANY] * 4 + [VM],
        [shape((128, 1024))] * 8, [ANY] * 8, [TOKENS, pltpu.VMEM((8, 128, 1024), BF)],
        16, 2 * 128 * 8192 * 256,
    )
    grad_token_in = scatter_ch(parts_in)
    grad_first, stats = call(
        grad_first_kernel, pre_all + [own_columns, first_normed],
        [ANY] * 2 + [VM] * 2, [shape((512, 256), F32), STATS], [VM] * 2,
        [HIDDEN], 16, 2 * 512 * 2048 * 256,
    )
    last_first, last_second = sum_ch(stats)
    grad_inputs = grad_middle + finish_adjoint(
        grad_first, first_normed, first_inverse, last_first, last_second
    )
    (grad_channel_in,) = call(
        widen_kernel, [grad_channel], [VM], [shape((128, 768), F32)], [VM], [], 1, 0
    )
    return (grad_inputs, grad_token_in, grad_token_out, grad_channel_in, grad_channel_out)


def solution(mesh):
    return jax.shard_map(
        body,
        mesh=mesh,
        in_specs=(
            P("tok", "ch"),
            P("tok", "ch"),
            P("tok", "ch"),
            P("tok", "ch"),
            P("tok", "ch"),
            P("ch", "tok"),
        ),
        out_specs=(P("tok", "ch"), P("tok", "ch"), P("tok", "ch"), P("tok", "ch"), P("ch", "tok")),
        check_vma=False,
    )
```

```python
import jax
import jax.numpy as jnp
from jax import lax
from jax.experimental import pallas as pl
from jax.experimental.pallas import tpu as pltpu
from jax.sharding import PartitionSpec as P


C = 2048
GELU_SCALE = 0.7978845608028654
CUBIC = 0.044715
EPSILON = 1e-05
BF = jnp.bfloat16
F32 = jnp.float32


def gelu_forward(value):
    inner = jnp.tanh(GELU_SCALE * (value + CUBIC * value * value * value))
    return 0.5 * value * (1.0 + inner)


def gelu_slope(value):
    inner = jnp.tanh(GELU_SCALE * (value + CUBIC * value * value * value))
    return 0.5 * (1.0 + inner) + 0.5 * value * (1.0 - inner * inner) * GELU_SCALE * (
        1.0 + 3.0 * CUBIC * value * value
    )


def finish_norm(values, total, total_sq):
    mean = total / C
    inverse = lax.rsqrt(total_sq / C - mean * mean + EPSILON)
    return ((values - mean[:, None]) * inverse[:, None], inverse)


def finish_adjoint(grad, normed, inverse, first_sum, second_sum):
    return inverse[:, None] * (grad - (first_sum / C)[:, None] - normed * (second_sum / C)[:, None])


def dot(left, right, left_dim=1, right_dim=0):
    return lax.dot_general(
        left, right, (((left_dim,), (right_dim,)), ((), ())), preferred_element_type=F32
    )


def ch_xor(x, k):
    return lax.ppermute(x, "ch", [(i, i ^ k) for i in range(8)])


def tok_xor(x, k):
    return lax.ppermute(x, "tok", [(i, i ^ k) for i in range(16)])


def relay(x, hop):
    near = hop(x, 1)
    blocks = [x, near] + [None] * 6
    for k in (2, 6, 4):
        blocks[k] = hop(x, k)
    for k in (2, 6, 4):
        blocks[k + 1] = hop(near, k)
    return blocks


def gather_ch(x):
    return relay(x, ch_xor)


def gather_tok(x, groups):
    blocks = relay(x, lambda v, j: tok_xor(v, 2 * j))
    stacks = []
    for group in groups:
        stacked = pack([blocks[j] for j in group])
        stacks += [stacked, tok_xor(stacked, 1)]
    return stacks


def scatter_ch(parts):
    moved = [None] * 8
    for k in (1, 2, 6, 3, 7, 4, 5):
        moved[k] = ch_xor(parts[k], k)
    total = parts[0].astype(F32)
    for k in range(1, 8):
        total = total + moved[k].astype(F32)
    return total


def scatter_ch_far_first(parts):
    moved = [None] * 4
    for i in (1, 3, 2):
        moved[i] = ch_xor(parts[i], 2 * i)
    total = parts[0].astype(F32)
    for i in range(1, 4):
        total = total + moved[i].astype(F32)
    got = ch_xor(total[1].astype(BF), 1)
    return total[0] + got.astype(F32)


def gather_small(copies):
    own = lax.all_to_all(copies, "tok", 0, 0, tiled=True, axis_index_groups=CHIPS)
    return [own, tok_xor(own, 1)]


CHIPS = [[2 * j + c for j in range(8)] for c in range(2)]


def reduce_tok(keep, send):
    got = tok_xor(send, 1)
    both = (keep.astype(F32) + got.astype(F32)).astype(BF)
    return lax.all_to_all(both, "tok", 0, 0, tiled=True, axis_index_groups=CHIPS)


def reduce_tok_far_first(keep, send):
    got = tok_xor(send, 1)
    both = [
        (keep[2 * i : 2 * i + 2].astype(F32) + got[2 * i : 2 * i + 2].astype(F32)).astype(BF)
        for i in range(4)
    ]
    moved = [None] * 4
    for i in (1, 3, 2):
        moved[i] = tok_xor(both[i], 4 * i)
    total = both[0].astype(F32)
    for i in range(1, 4):
        total = total + moved[i].astype(F32)
    other = tok_xor(total[1].astype(BF), 2)
    return total[0] + other.astype(F32)


def sum_ch(stats):
    moved = lax.all_to_all(stats, "ch", 0, 0, tiled=True)
    total = jnp.sum(moved, axis=0)
    return total[0], total[1]


ANY = pl.BlockSpec(memory_space=pl.ANY)
VM = pl.BlockSpec(memory_space=pltpu.VMEM)


def call(kernel, ins, in_specs, outs, out_specs, scratch, n_copies, flops):
    moved = sum(x.size * x.dtype.itemsize for x in ins) + sum(
        o.size * o.dtype.itemsize for o in outs
    )
    return pl.pallas_call(
        kernel,
        out_shape=outs,
        in_specs=in_specs,
        out_specs=out_specs,
        scratch_shapes=list(scratch) + [pltpu.SemaphoreType.DMA((n_copies,))],
        cost_estimate=pl.CostEstimate(flops=flops, bytes_accessed=moved, transcendentals=0),
    )(*ins)


def where_am_i():
    me = lax.axis_index("ch")
    tok = lax.axis_index("tok")
    return me, tok // 2, tok % 2


def start(pairs, sems, first=0):
    copies = [
        pltpu.make_async_copy(src, dst, sems.at[first + n]) for n, (src, dst) in enumerate(pairs)
    ]
    for copy in copies:
        copy.start()
    return copies


def fetch(pairs, sems):
    for copy in start(pairs, sems):
        copy.wait()


def ch_pairs(blocks, scratch, me):
    return [(blocks[k], scratch.at[me ^ k]) for k in range(8)]


def back_pairs(scratch, blocks, me):
    return [(scratch.at[me ^ k], blocks[k]) for k in range(8)]


def back_twos(scratch, blocks, me):
    return [(scratch.at[me ^ k], blocks[k // 2].at[k % 2]) for k in range(8)]


def pack_kernel(*refs):
    for n, ref in enumerate(refs[:-2]):
        refs[-2][n] = ref[...]


def pack(blocks):
    out = shape((len(blocks),) + blocks[0].shape)
    return call(pack_kernel, blocks, [VM] * len(blocks), [out], [VM], [], 1, 0)[0]


def weights_kernel(in_ref, out_ref, both_ref, sems):
    both_ref[:, :768] = in_ref[...]
    both_ref[:, 768:] = out_ref[...].T


def ch_column_pairs(blocks, scratch, me):
    return [
        (blocks[k].at[pl.ds(0, 512)], scratch.at[:, pl.ds(pl.multiple_of((me ^ k) * 256, 256), 256)])
        for k in range(8)
    ]


FIRST_GROUPS = ((0, 2, 6, 4), (1, 3, 7, 5))


def small_pairs(stacks, scratch, core):
    return [
        (stacks[s].at[j], scratch.at[2 * j + (core ^ s)]) for s in range(2) for j in range(8)
    ]


def tok_pairs(stacks, groups, scratch, pair, core):
    return [
        (stacks[2 * n + s].at[i], scratch.at[(pair ^ j) * 2 + (core ^ s)])
        for n, group in enumerate(groups)
        for s in range(2)
        for i, j in enumerate(group)
    ]


def row_sums(value):
    ones = jnp.ones((256, 128), BF)
    total = jnp.zeros((512, 128), F32)
    for _ in range(3):
        part = value.astype(BF)
        value = value - part.astype(F32)
        total = total + dot(part, ones)
    return total


def put_rows(ref, first, second):
    lane = lax.broadcasted_iota(jnp.int32, (512, 128), 1)
    block = jnp.where(lane == 0, first, second).T[:8]
    for c in range(8):
        ref[c] = block


def as_tail(first, second):
    lane = lax.broadcasted_iota(jnp.int32, (512, 128), 1)
    value = jnp.where(lane % 2 == 0, first, second).T[:8]
    high = value.astype(BF).astype(F32)
    mid = (value - high).astype(BF).astype(F32)
    row = lax.broadcasted_iota(jnp.int32, (8, 512), 0)
    terms = jnp.where(row < 2, high, jnp.where(row < 4, mid, value - high - mid))
    return jnp.concatenate([terms[:, :256], terms[:, 256:]]).astype(BF)


def from_tail(tail):
    tail = tail.astype(F32)

    def row(n):
        halves = [
            tail[..., at, :] + tail[..., at + 2, :] + tail[..., at + 4, :] for at in (n, n + 8)
        ]
        return jnp.concatenate(halves, axis=-1)

    return row(0), row(1)


def put_stats(ref, first, second):
    put_rows(ref, row_sums(first), row_sums(second))


def input_stats_kernel(inputs_ref, stats_ref, sems):
    value = inputs_ref[...]
    put_stats(stats_ref, value, value * value)


def token_pre_kernel(*refs):
    rows, normed = refs[:8], refs[8:12]
    pre_ref, act_ref, blocks_ref, row_all, normed_all, sems = refs[12:]
    me, pair, core = where_am_i()
    fetch(
        ch_pairs(rows, row_all, me) + tok_pairs(normed, FIRST_GROUPS, normed_all, pair, core), sems
    )
    copies = start(
        [
            (row_all.at[t // 2, :, pl.ds(t % 2 * 512, 512)], blocks_ref.at[t])
            for t in range(16)
        ],
        sems,
    )
    total = jnp.zeros((128, 256), F32)
    for c in range(8):
        total = total + dot(row_all[c], normed_all[2 * c : 2 * c + 2].reshape(1024, 256))
    pre_ref[...] = total
    act = gelu_forward(total).astype(BF)
    for j in range(8):
        act_ref[j] = act
    for copy in copies:
        copy.wait()


def middle_kernel(*refs):
    out_blocks, act_blocks, inputs_ref = refs[:8], refs[8:10], refs[10]
    middle_ref, apart_ref, out_all, act_all, sems = refs[11:]
    me, _, core = where_am_i()
    fetch(
        ch_column_pairs(out_blocks, out_all, me)
        + small_pairs(act_blocks, act_all, core),
        sems,
    )
    middle = inputs_ref[...] + dot(out_all[...], act_all[...].reshape(2048, 256))
    middle_ref[...] = middle
    mean = row_sums(middle) * (1.0 / 256)
    apart = middle - jnp.concatenate([mean, mean], axis=1)
    apart_ref[:512] = apart.astype(BF)
    apart_ref[512:] = as_tail(mean, row_sums(apart * apart))


def merge_stats(means, squares):
    mean = jnp.sum(means, axis=0, keepdims=True) * (1.0 / 8)
    apart = means - mean
    total = jnp.sum(squares + 256.0 * apart * apart, axis=0, keepdims=True)
    return mean, lax.rsqrt(total / C + EPSILON)


def grad_act_kernel(*refs):
    grads, weights, out_ref, grad_all, weight_all, sems = refs[:8], *refs[8:]
    me, _, _ = where_am_i()
    fetch(
        ch_column_pairs(grads, grad_all, me) + [(weights.at[:, pl.ds(768, 768)], weight_all)],
        sems,
    )
    for h in range(3):
        cols = slice(256 * h, 256 * h + 256)
        out_ref[:, cols] = dot(grad_all[...], weight_all[:, cols])


def channel_kernel(*refs):
    apart, weights, grad_act = refs[:8], refs[8], refs[9]
    act_out, pre_out, normed_out, merged_ref = refs[10:14]
    parts = refs[14:22]
    weight_all, first_sum, second_sum, part_all = refs[22:26]
    normed_all, grad_act_ref, act_ref, pre_ref, tails, tail_out, sems = refs[26:]
    me, _, _ = where_am_i()
    first_copies = start(
        [(apart[k].at[pl.ds(512, 16)], tails.at[me ^ k]) for k in range(8)], sems, 13
    )
    copies = start(ch_column_pairs(apart, normed_all, me), sems)
    later = start(
        [(weights.at[:, pl.ds(0, 768)], weight_all), (grad_act, grad_act_ref)], sems, 8
    )
    for copy in first_copies:
        copy.wait()
    means, squares = from_tail(tails[...])
    mean, inverse = merge_stats(means, squares)
    merged_ref[...] = jnp.concatenate([mean, inverse, jnp.zeros((6, 512), F32)])
    rows = jnp.concatenate(
        [means - mean, jnp.broadcast_to(inverse, (8, 512)), jnp.zeros((112, 512), F32)]
    ).T
    inverse = jnp.broadcast_to(rows[:, 8:9], (512, 256))
    for copy in copies:
        copy.wait()
    for c in range(8):
        cols = slice(256 * c, 256 * c + 256)
        value = normed_all[:, cols].astype(F32) + jnp.broadcast_to(rows[:, c : c + 1], (512, 256))
        normed_all[:, cols] = (value * inverse).astype(BF)
    out_copies = start([(normed_all, normed_out)], sems, 10)
    for copy in later:
        copy.wait()

    def hidden(h, carry):
        cols = pl.ds(pl.multiple_of(256 * h, 256), 256)
        pre = dot(normed_all[...], weight_all[:, cols])
        act_ref[:, cols] = gelu_forward(pre).astype(BF)
        pre_ref[:, cols] = (grad_act_ref[:, cols] * gelu_slope(pre)).astype(BF)
        return carry

    lax.fori_loop(0, 3, hidden, 0)
    out_copies += start([(act_ref, act_out), (pre_ref, pre_out)], sems, 11)
    first_sum[...] = jnp.zeros((512, 256), F32)
    second_sum[...] = jnp.zeros((512, 256), F32)

    def part(c, carry):
        rows = pl.ds(pl.multiple_of(c * 256, 256), 256)
        value = dot(pre_ref[...], weight_all[rows, :], 1, 1).astype(BF)
        part_all[c] = value
        value = value.astype(F32)
        first_sum[...] += value
        second_sum[...] += value * normed_all[:, rows].astype(F32)
        return carry

    lax.fori_loop(0, 8, part, 0)
    copies = start(
        [(part_all.at[me ^ k], parts[k].at[pl.ds(0, 512)]) for k in range(8)], sems
    )
    tail_out[...] = as_tail(row_sums(first_sum[...]), row_sums(second_sum[...]))
    copies += start([(tail_out, parts[k].at[pl.ds(512, 16)]) for k in range(8)], sems, 13)
    for copy in copies + out_copies:
        copy.wait()


def channel_grad_kernel(*refs):
    grads, normed_ref = refs[:8], refs[8]
    act_ref, pre_ref, in_out, keep_out, send_out, grad_all = refs[9:15]
    in_ref, keep_ref, send_ref, sems = refs[15:]
    me, pair, core = where_am_i()
    fetch(ch_pairs(grads, grad_all, me), sems)
    first = core == 0

    def step(c, carry):
        rows = pl.ds(pl.multiple_of(c * 256, 256), 256)
        in_ref[c] = dot(normed_ref[:, rows], pre_ref[...], 0, 0).astype(BF)
        block = dot(grad_all[c], act_ref[...], 0, 0)
        low, high = block[:128], block[128:]
        keep_ref[c] = jnp.where(first, low, high).astype(BF)
        send_ref[c] = jnp.where(first, high, low).astype(BF)
        for copy in leaving(c):
            copy.start()
        return carry

    def leaving(c):
        rows = pl.ds(pl.multiple_of(c * 256, 256), 256)
        return [
            pltpu.make_async_copy(in_ref.at[c], in_out.at[rows], sems.at[8 + c]),
            pltpu.make_async_copy(keep_ref.at[c], keep_out.at[c ^ pair], sems.at[16 + c]),
            pltpu.make_async_copy(send_ref.at[c], send_out.at[c ^ pair], sems.at[24 + c]),
        ]

    lax.fori_loop(0, 8, step, 0)
    for c in range(8):
        for copy in leaving(c):
            copy.wait()


def widen_kernel(in_ref, out_ref, sems):
    out_ref[...] = in_ref[...].astype(F32)


def keep_kernel(in_ref, out_ref, sems):
    out_ref[...] = in_ref[...]


def token_act_grad_kernel(*refs):
    out_blocks, middle_ref = refs[:8], refs[8]
    keep_ref, send_ref, out_all, sems = refs[9:]
    me, _, core = where_am_i()
    fetch(ch_pairs(out_blocks, out_all, me), sems)

    first = core == 0
    for c in range(8):
        block = dot(out_all[c], middle_ref[...], 0, 0).astype(BF)
        low, high = block[:128], block[128:]
        keep_ref[c] = jnp.where(first, low, high)
        send_ref[c] = jnp.where(first, high, low)


def token_grad_kernel(moved_ref, pre_ref, out_ref, sems):
    total = moved_ref[0].astype(F32)
    for j in range(1, 8):
        total = total + moved_ref[j].astype(F32)
    value = (total * gelu_slope(pre_ref[...])).astype(BF)
    for j in range(8):
        out_ref[j] = value


def token_out_kernel(*refs):
    act_blocks, middle_ref = refs[:2], refs[2]
    parts = refs[3:7]
    act_all, part_all, sems = refs[7:]
    me, _, core = where_am_i()
    fetch(small_pairs(act_blocks, act_all, core), sems)

    for c in range(8):
        block = act_all[2 * c : 2 * c + 2].reshape(256, 256)
        part_all[c] = dot(middle_ref[...], block, 1, 1).astype(BF)
    fetch(back_twos(part_all, parts, me), sems)


def token_in_kernel(*refs):
    normed, grad_ref = refs[:4], refs[4]
    parts = refs[5:13]
    normed_all, part_all, sems = refs[13:]
    me, pair, core = where_am_i()
    fetch(tok_pairs(normed, FIRST_GROUPS, normed_all, pair, core), sems)

    for c in range(8):
        block = normed_all[2 * c : 2 * c + 2].reshape(1024, 256)
        part_all[c] = dot(grad_ref[0], block, 1, 1).astype(BF)
    fetch(back_pairs(part_all, parts, me), sems)


def grad_first_kernel(*refs):
    grads, column_ref, normed_ref = refs[:2], refs[2], refs[3]
    out_ref, stats_ref, grad_all, sems = refs[4:]
    _, _, core = where_am_i()
    fetch(small_pairs(grads, grad_all, core), sems)
    total = dot(column_ref[...], grad_all[...].reshape(2048, 256), 0, 0)
    out_ref[...] = total
    put_stats(stats_ref, total, total * normed_ref[...])


def shape(dims, dtype=BF):
    return jax.ShapeDtypeStruct(dims, dtype)


STATS = shape((8, 8, 512), F32)
WIDE = pltpu.VMEM((512, 2048), BF)
EIGHT = pltpu.VMEM((8, 512, 256), BF)
HIDDEN = pltpu.VMEM((16, 128, 256), BF)
TOKENS = pltpu.VMEM((16, 512, 256), BF)


def body(inputs, cotangent, token_in, token_out, channel_in, channel_out):
    (stats,) = call(input_stats_kernel, [inputs], [VM], [STATS], [VM], [], 1, 2 * 10**6)
    row_total, row_square = sum_ch(stats)
    first_normed, first_inverse = finish_norm(inputs, row_total, row_square)
    normed_cols = gather_tok(first_normed.astype(BF), FIRST_GROUPS)
    in_rows = gather_ch(token_in)
    out_rows = gather_ch(token_out)
    grad_wide = gather_ch(cotangent.astype(BF))

    (own_weights,) = call(
        weights_kernel, [channel_in, channel_out], [VM] * 2,
        [shape((128, 1536))], [VM], [], 1, 0,
    )
    weights = lax.all_gather(own_weights, "tok", axis=0, tiled=True)

    token_pre, token_act, row_blocks = call(
        token_pre_kernel, in_rows + normed_cols, [ANY] * 12,
        [shape((128, 256), F32), shape((8, 128, 256)), shape((16, 128, 512))], [VM] * 2 + [ANY],
        [pltpu.VMEM((8, 128, 1024), BF), TOKENS], 24, 2 * 128 * 8192 * 256,
    )
    acts = gather_small(token_act)
    middle, apart = call(
        middle_kernel, out_rows + acts + [inputs], [ANY] * 10 + [VM],
        [shape((512, 256), F32), shape((528, 256))], [VM] * 2, [WIDE, HIDDEN],
        24, 2 * 512 * 2048 * 256,
    )
    own_columns = lax.all_to_all(row_blocks, "tok", 0, 0, tiled=True).reshape(2048, 512)
    apart_wide = gather_ch(apart)
    (grad_act,) = call(
        grad_act_kernel, grad_wide + [weights], [ANY] * 9,
        [shape((512, 768), F32)], [VM], [WIDE, pltpu.VMEM((2048, 768), BF)],
        9, 2 * 512 * 2048 * 768,
    )
    results = call(
        channel_kernel, apart_wide + [weights, grad_act], [ANY] * 10,
        [shape((512, 768)), shape((512, 768)), shape((512, 2048)), shape((8, 512), F32)]
        + [shape((528, 256))] * 8,
        [ANY] * 3 + [VM] + [ANY] * 8,
        [pltpu.VMEM((2048, 768), BF)] + [pltpu.VMEM((512, 256), F32)] * 2
        + [EIGHT, WIDE, pltpu.VMEM((512, 768), F32)] + [pltpu.VMEM((512, 768), BF)] * 2
        + [pltpu.VMEM((8, 16, 256), BF), pltpu.VMEM((16, 256), BF)],
        21, 4 * 512 * 2048 * 768,
    )
    channel_act, grad_pre, normed_wide, merged = results[:4]
    total_second = scatter_ch(results[4:])
    grad_second = total_second[:512]
    adj_first, adj_second = from_tail(total_second[512:])
    part_in_all, keep_channel, send_channel = call(
        channel_grad_kernel,
        grad_wide + [normed_wide, channel_act, grad_pre], [ANY] * 8 + [VM] * 3,
        [shape((2048, 768))] + [shape((8, 128, 768))] * 2, [ANY] * 3,
        [EIGHT, pltpu.VMEM((8, 256, 768), BF)] + [pltpu.VMEM((8, 128, 768), BF)] * 2,
        32, 4 * 512 * 2048 * 768,
    )
    grad_channel = lax.psum_scatter(part_in_all, "tok", scatter_dimension=0, tiled=True)
    grad_channel_out = reduce_tok_far_first(keep_channel, send_channel).T
    (merged,) = call(keep_kernel, [merged], [VM], [shape((8, 512), F32)], [VM], [], 1, 0)
    second_inverse = merged[1]
    second_normed = (middle - merged[0][:, None]) * second_inverse[:, None]
    grad_middle = cotangent + finish_adjoint(
        grad_second, second_normed, second_inverse, adj_first, adj_second
    )
    middle_rounded = grad_middle.astype(BF)
    keep, send = call(
        token_act_grad_kernel, out_rows + [middle_rounded], [ANY] * 8 + [VM],
        [shape((8, 128, 256))] * 2, [VM] * 2, [EIGHT], 8, 2 * 512 * 2048 * 256,
    )
    grad_token_act = reduce_tok(keep, send)
    parts_out = call(
        token_out_kernel, acts + [middle_rounded], [ANY] * 2 + [VM],
        [shape((2, 512, 256))] * 4, [ANY] * 4, [HIDDEN, EIGHT], 16, 2 * 512 * 2048 * 256,
    )
    grad_token_out = scatter_ch_far_first(parts_out)
    (token_grad_pre,) = call(
        token_grad_kernel, [grad_token_act, token_pre], [VM] * 2,
        [shape((8, 128, 256))], [VM], [], 1, 0,
    )
    pre_all = gather_small(token_grad_pre)
    parts_in = call(
        token_in_kernel, normed_cols + [token_grad_pre], [ANY] * 4 + [VM],
        [shape((128, 1024))] * 8, [ANY] * 8, [TOKENS, pltpu.VMEM((8, 128, 1024), BF)],
        16, 2 * 128 * 8192 * 256,
    )
    grad_token_in = scatter_ch(parts_in)
    grad_first, stats = call(
        grad_first_kernel, pre_all + [own_columns, first_normed],
        [ANY] * 2 + [VM] * 2, [shape((512, 256), F32), STATS], [VM] * 2,
        [HIDDEN], 16, 2 * 512 * 2048 * 256,
    )
    last_first, last_second = sum_ch(stats)
    grad_inputs = grad_middle + finish_adjoint(
        grad_first, first_normed, first_inverse, last_first, last_second
    )
    (grad_channel_in,) = call(
        widen_kernel, [grad_channel], [VM], [shape((128, 768), F32)], [VM], [], 1, 0
    )
    return (grad_inputs, grad_token_in, grad_token_out, grad_channel_in, grad_channel_out)


def solution(mesh):
    return jax.shard_map(
        body,
        mesh=mesh,
        in_specs=(
            P("tok", "ch"),
            P("tok", "ch"),
            P("tok", "ch"),
            P("tok", "ch"),
            P("tok", "ch"),
            P("ch", "tok"),
        ),
        out_specs=(P("tok", "ch"), P("tok", "ch"), P("tok", "ch"), P("tok", "ch"), P("ch", "tok")),
        check_vma=False,
    )
```
